512 devices in a mesh: tok: 16 (over z), blk: 32 (over y, x, core).
Axes of the slice: x: 4, y: 4, z: 16, core: 2. Of those that a mesh axis runs over, the one named last changes fastest.
Arguments:
- acts: bfloat16 [2048, 8192], P('tok', 'blk'), may hold values from -35 to 35
- out_grad: bfloat16 [2048, 29568], P(('tok', 'blk')), may hold values from -0.12 to 0.12
- kept_ids: int32 [32, 16], replicated, may hold values from 0 to 14783, as said below
- cand_ids: int32 [32, 48], replicated, may hold values from 0 to 14783, as said below
Outputs:
- kept_grad: bfloat16 [32, 16, 128, 128], P('blk', 'tok')
- cand_score: float32 [32, 48], P('blk', 'tok')
The draws below stay inside these ranges and needn't reach their ends.
Inputs may be any that keep to these rules, and one draw needn't show every extreme that they name: `kept_ids`: within one owner's kept and candidate blocks every block id appears once; one owner's blocks use at most 16 distinct block columns, exactly 16 for some owner, and no block column is used by two owners. `cand_ids`: numbered and owned as the kept blocks, and distinct from them.
All inputs are finite; a program needn't handle non-finite values.
Results may differ from the reference program's by a relative error of at most 0.001.
Values may be sent and summed in bfloat16 or wider, within the bound.
A program may use at most 64 MiB of HBM per device.

```python
import math
import jax
import jax.numpy as jnp
from jax import lax

D = 8192
F = 29568
BLOCK = 128
TOK_DEV = 128
KS = 16
CS = 48
TOKENS = 2048
NRB = 64
NCB = 231
BLOCK_HOLDERS = 32
MC = 16


def owner_table(key):
    key_cols, key_owner = jax.random.split(key)
    col_order = jax.random.permutation(key_cols, NCB)
    owner_order = jax.random.permutation(key_owner, BLOCK_HOLDERS)
    position = jnp.arange(NCB)
    first = MC + 2 * (BLOCK_HOLDERS - 1)
    slot = jnp.where(position < MC, 0, jnp.where(position < first, 1 + (position - MC) // 2, 1 + (position - first) % (BLOCK_HOLDERS - 1)))
    owner_at = owner_order[slot]
    return jnp.zeros((NCB,), jnp.int32).at[col_order].set(owner_at.astype(jnp.int32))


def block_lists(key):
    col_owner = owner_table(jax.random.fold_in(key, 1))
    ranking_score = jax.random.fold_in(key, 2)
    key_row = jax.random.fold_in(key, 3)
    grand_total = NRB * NCB
    entry_index = jnp.arange(grand_total)
    block_column_index = entry_index % NCB
    block_row_index = entry_index // NCB
    selected_row = jax.random.randint(key_row, (NCB,), 0, NRB)
    extra_score = jnp.where(block_row_index == selected_row[block_column_index], 1 << 30, 0)
    base_offset = jax.random.randint(ranking_score, (BLOCK_HOLDERS, grand_total), 0, 32768) * grand_total + entry_index[None, :] + extra_score[None, :]
    owned = col_owner[block_column_index][None, :] == jnp.arange(BLOCK_HOLDERS)[:, None]
    scores = jnp.where(owned, base_offset, -1 - entry_index[None, :])
    chosen = jax.lax.top_k(scores, KS + CS)[1].astype(jnp.int32)
    return chosen


def draw_kept_ids(key, part):
    return block_lists(key)[:, :KS]


def draw_cand_ids(key, part):
    return block_lists(key)[:, KS:]


def feature_scales(key, count, low, ratio):
    key_block, key_rough = jax.random.split(key)
    block_scale = low * jnp.exp(math.log(ratio) * jax.random.uniform(key_block, (count // BLOCK, 1)))
    rough = jnp.exp(math.log(2.0) * (jax.random.uniform(key_rough, (count // BLOCK, BLOCK)) - 0.5))
    return (block_scale * rough).reshape(count)


def draw_acts(key, part):
    key_val, key_scale = jax.random.split(key)
    values = jnp.clip(jax.random.normal(key_val, (TOKENS, D)), -5.0, 5.0)
    scales = feature_scales(key_scale, D, 0.5, 10.0)
    return (values * scales[None, :]).astype(jnp.bfloat16)


def draw_out_grad(key, part):
    key_val, key_scale = jax.random.split(key)
    values = jnp.clip(jax.random.normal(key_val, (TOKENS, F)), -5.0, 5.0)
    scales = feature_scales(key_scale, F, 0.7071, 2.0)
    return (values * scales[None, :] * 0.011).astype(jnp.bfloat16)


def setup_inputs(seed: int = 0) -> dict:
    streams_of = jax.random.split(jax.random.key(seed), 5)
    acts = draw_acts(jax.random.fold_in(streams_of[4], 71), 0)
    out_grad = draw_out_grad(jax.random.fold_in(streams_of[4], 71), 0)
    kept_ids = draw_kept_ids(jax.random.fold_in(streams_of[4], 71), 0)
    cand_ids = draw_cand_ids(jax.random.fold_in(streams_of[4], 71), 0)
    return {"acts": acts, "out_grad": out_grad, "kept_ids": kept_ids, "cand_ids": cand_ids}


def block_gradient(acts3, grad3, block_id):
    row = (block_id // NCB).astype(jnp.int32)
    col = (block_id % NCB).astype(jnp.int32)
    left = lax.dynamic_slice_in_dim(acts3, row * BLOCK, BLOCK, 2).astype(jnp.float32)
    right = lax.dynamic_slice_in_dim(grad3, col * BLOCK, BLOCK, 2).astype(jnp.float32)
    partial_value = jnp.einsum('gti,gtj->gij', left, right)
    return lax.optimization_barrier(jnp.sum(partial_value, axis=0))

def reference(acts, out_grad, kept_ids, cand_ids):
    groups = acts.shape[0] // TOK_DEV
    acts3 = acts.reshape(groups, TOK_DEV, D)
    grad3 = out_grad.reshape(groups, TOK_DEV, F)

    def one_block(block_id):
        return block_gradient(acts3, grad3, block_id)
    kept_blocks = lax.map(one_block, kept_ids.reshape(-1))
    cand_blocks = lax.map(one_block, cand_ids.reshape(-1))
    kept_grad = kept_blocks.astype(jnp.bfloat16).reshape(BLOCK_HOLDERS, KS, BLOCK, BLOCK)
    norms = jnp.sqrt(lax.optimization_barrier(jnp.sum(cand_blocks * cand_blocks, axis=(1, 2))))
    peak = jnp.max(norms)
    cand_score = (norms / (peak + 1e-06)).reshape(BLOCK_HOLDERS, CS)
    return (kept_grad, cand_score)
```

```python
import jax
import jax.numpy as jnp
from jax import lax
from jax.experimental import pallas as pl
from jax.experimental.pallas import tpu as pltpu
from jax.sharding import PartitionSpec as P

BLOCK = 128
KS = 16


def column_tables(cols, width):
    slots = cols.shape[1]
    same = cols[:, :, None] == cols[:, None, :]
    place = jnp.arange(slots)
    earlier = place[None, :] < place[:, None]
    first = jnp.logical_not(jnp.any(same & earlier[None], axis=2))
    rank = jnp.sum(jnp.where(earlier[None] & first[:, None, :], 1, 0), axis=2)
    position = jnp.sum(jnp.where(same & first[:, None, :], rank[:, None, :], 0), axis=2)
    hit = first[:, None, :] & (rank[:, None, :] == jnp.arange(width)[None, :, None])
    table = jnp.sum(jnp.where(hit, cols[:, None, :], 0), axis=2)
    return table.astype(jnp.int32), position.astype(jnp.int32)


def pick_kernel(owners, width, table_ref, grad_ref, out_ref):
    def one_owner(o, carry):
        for w in range(width):
            col = table_ref[o * width + w]
            out_ref[o, :, w * BLOCK : (w + 1) * BLOCK] = grad_ref[
                :, pl.ds(pl.multiple_of(col * BLOCK, BLOCK), BLOCK)
            ]
        return carry

    lax.fori_loop(0, owners, one_owner, 0)


def product_kernel(per, rows_ref, cols_ref, acts_ref, grad_ref, kept_ref, cand_ref):
    def product(slot):
        row = rows_ref[slot]
        col = cols_ref[slot]
        left = acts_ref[row // per, :, pl.ds(pl.multiple_of((row % per) * BLOCK, BLOCK), BLOCK)]
        right = grad_ref[:, pl.ds(pl.multiple_of(col * BLOCK, BLOCK), BLOCK)]
        return lax.dot_general(
            left, right, (((0,), (0,)), ((), ())), preferred_element_type=jnp.float32
        )

    def kept(j, carry):
        for u in range(4):
            kept_ref[4 * j + u] = product(4 * j + u)
        return carry

    def cand(j, carry):
        for u in range(4):
            cand_ref[4 * j + u] = product(kept_ref.shape[0] + 4 * j + u).astype(cand_ref.dtype)
        return carry

    lax.fori_loop(0, kept_ref.shape[0] // 4, kept, 0)
    lax.fori_loop(0, cand_ref.shape[0] // 4, cand, 0)


def score_kernel(norm_ref, score_ref, line, plane, own_sem, line_send, line_recv, plane_send, plane_recv):
    nt, nb = lax.axis_size("tok"), lax.axis_size("blk")
    t, b = lax.axis_index("tok"), lax.axis_index("blk")
    barrier = pltpu.get_barrier_semaphore()

    def greet(axis, me, n):
        def one(k, carry):
            pl.semaphore_signal(
                barrier, inc=1, device_id={axis: lax.rem(me + k, n)}, device_id_type=pl.DeviceIdType.MESH
            )
            return carry

        lax.fori_loop(1, n, one, 0)

    greet("tok", t, nt)
    greet("blk", b, nb)
    pl.semaphore_wait(barrier, nt + nb - 2)

    def exchange(axis, me, n, src, buf, send, recv):
        def copy(k, slot):
            return pltpu.make_async_remote_copy(
                src_ref=src,
                dst_ref=buf.at[slot],
                send_sem=send.at[k],
                recv_sem=recv.at[k],
                device_id={axis: lax.rem(me + k, n)},
                device_id_type=pl.DeviceIdType.MESH,
            )

        def start(k, carry):
            copy(k, me).start()
            return carry

        def finish(k, carry):
            arrived = copy(k, lax.rem(me + n - k, n))
            arrived.wait_send()
            arrived.wait_recv()
            return carry

        lax.fori_loop(1, n, start, 0)
        own = pltpu.make_async_copy(src, buf.at[me], own_sem)
        own.start()
        own.wait()
        lax.fori_loop(1, n, finish, 0)

    exchange("tok", t, nt, norm_ref, line, line_send, line_recv)
    exchange("blk", b, nb, line, plane, plane_send, plane_recv)
    peak = jnp.max(plane[...])
    score_ref[...] = norm_ref[...] / (peak + 1e-06)


def local(acts, out_grad, kept_ids, cand_ids):
    owners = lax.axis_size("blk")
    owner_index = lax.axis_index("blk")
    ncols = out_grad.shape[1] // BLOCK
    width = 2 * ((ncols + owners - 1) // owners)
    tokens = acts.shape[0]
    per = acts.shape[1] // BLOCK
    slot_ids = jnp.concatenate([kept_ids, cand_ids], axis=1)
    acts_all = lax.all_gather(acts, "blk", axis=0, tiled=False)
    table, position = column_tables(slot_ids % ncols, width)
    vmem = pl.BlockSpec(memory_space=pltpu.VMEM)
    smem = pl.BlockSpec(memory_space=pltpu.SMEM)
    outgoing = pl.pallas_call(
        lambda *refs: pick_kernel(owners, width, *refs),
        out_shape=jax.ShapeDtypeStruct((owners, out_grad.shape[0], width * BLOCK), out_grad.dtype),
        in_specs=[smem, vmem],
        out_specs=vmem,
        name="pick",
    )(table.reshape(-1), out_grad)
    incoming = lax.all_to_all(outgoing, "blk", split_axis=0, concat_axis=0, tiled=True)
    grad_cols = incoming.reshape(tokens, width * BLOCK)
    my_rows = lax.dynamic_index_in_dim(slot_ids // ncols, owner_index, 0, keepdims=False)
    my_cols = lax.dynamic_index_in_dim(position, owner_index, 0, keepdims=False)
    kept_part, cand_part = pl.pallas_call(
        lambda *refs: product_kernel(per, *refs),
        out_shape=(
            jax.ShapeDtypeStruct((KS, BLOCK, BLOCK), jnp.float32),
            jax.ShapeDtypeStruct((cand_ids.shape[1], BLOCK, BLOCK), jnp.bfloat16),
        ),
        in_specs=[smem, smem, vmem, vmem],
        out_specs=(vmem, vmem),
        name="products",
    )(my_rows, my_cols, acts_all, grad_cols)
    cand_sum = lax.psum_scatter(cand_part, "tok", scatter_dimension=0, tiled=True)
    kept_sum = lax.psum_scatter(kept_part, "tok", scatter_dimension=0, tiled=True)
    kept_grad = kept_sum.astype(jnp.bfloat16)[None]
    cand_sum = cand_sum.astype(jnp.float32)
    norms = jnp.sqrt(jnp.sum(cand_sum * cand_sum, axis=(1, 2)))
    toks = lax.axis_size("tok")
    share = norms.shape[0]
    dma = pltpu.SemaphoreType.DMA
    scores = pl.pallas_call(
        score_kernel,
        out_shape=jax.ShapeDtypeStruct((1, BLOCK), jnp.float32),
        in_specs=[vmem],
        out_specs=vmem,
        scratch_shapes=[
            pltpu.VMEM((toks, 1, BLOCK), jnp.float32),
            pltpu.VMEM((owners, toks, 1, BLOCK), jnp.float32),
            dma,
            dma((toks,)),
            dma((toks,)),
            dma((owners,)),
            dma((owners,)),
        ],
        compiler_params=pltpu.CompilerParams(collective_id=0, has_side_effects=True),
        name="scores",
    )(jnp.pad(norms, (0, BLOCK - share))[None])
    cand_score = scores[:, :share]
    return (kept_grad, cand_score)


def solution(mesh):
    return jax.shard_map(
        local,
        mesh=mesh,
        in_specs=(P("tok", "blk"), P(("tok", "blk"), None), P(), P()),
        out_specs=(P("blk", "tok", None, None), P("blk", "tok")),
        check_vma=False,
    )
```

```python
import jax
import jax.numpy as jnp
from jax import lax
from jax.experimental import pallas as pl
from jax.experimental.pallas import tpu as pltpu
from jax.sharding import PartitionSpec as P

BLOCK = 128
KS = 16


def column_tables(cols, width):
    slots = cols.shape[1]
    same = cols[:, :, None] == cols[:, None, :]
    place = jnp.arange(slots)
    earlier = place[None, :] < place[:, None]
    first = jnp.logical_not(jnp.any(same & earlier[None], axis=2))
    rank = jnp.sum(jnp.where(earlier[None] & first[:, None, :], 1, 0), axis=2)
    position = jnp.sum(jnp.where(same & first[:, None, :], rank[:, None, :], 0), axis=2)
    hit = first[:, None, :] & (rank[:, None, :] == jnp.arange(width)[None, :, None])
    table = jnp.sum(jnp.where(hit, cols[:, None, :], 0), axis=2)
    return table.astype(jnp.int32), position.astype(jnp.int32)


def pick_kernel(owners, width, table_ref, grad_ref, out_ref):
    def one_owner(o, carry):
        for w in range(width):
            col = table_ref[o * width + w]
            out_ref[o, :, w * BLOCK : (w + 1) * BLOCK] = grad_ref[
                :, pl.ds(pl.multiple_of(col * BLOCK, BLOCK), BLOCK)
            ]
        return carry

    lax.fori_loop(0, owners, one_owner, 0)


def product_kernel(per, rows_ref, cols_ref, acts_ref, grad_ref, kept_ref, cand_ref):
    def product(slot):
        row = rows_ref[slot]
        col = cols_ref[slot]
        left = acts_ref[row // per, :, pl.ds(pl.multiple_of((row % per) * BLOCK, BLOCK), BLOCK)]
        right = grad_ref[:, pl.ds(pl.multiple_of(col * BLOCK, BLOCK), BLOCK)]
        return lax.dot_general(
            left, right, (((0,), (0,)), ((), ())), preferred_element_type=jnp.float32
        )

    def kept(j, carry):
        for u in range(4):
            kept_ref[4 * j + u] = product(4 * j + u)
        return carry

    def cand(j, carry):
        for u in range(4):
            cand_ref[4 * j + u] = product(kept_ref.shape[0] + 4 * j + u).astype(cand_ref.dtype)
        return carry

    lax.fori_loop(0, kept_ref.shape[0] // 4, kept, 0)
    lax.fori_loop(0, cand_ref.shape[0] // 4, cand, 0)


MESH = pl.DeviceIdType.MESH


def greet(barrier, axis, me, n):
    def one(k, carry):
        pl.semaphore_signal(
            barrier, inc=1, device_id={axis: lax.rem(me + k, n)}, device_id_type=MESH
        )
        return carry

    lax.fori_loop(1, n, one, 0)


def exchange(axis, me, n, src, buf, send, recv, own_sem):
    def copy(k, slot):
        return pltpu.make_async_remote_copy(
            src_ref=src,
            dst_ref=buf.at[slot],
            send_sem=send.at[k],
            recv_sem=recv.at[k],
            device_id={axis: lax.rem(me + k, n)},
            device_id_type=MESH,
        )

    def start(k, carry):
        copy(k, me).start()
        return carry

    def finish(k, carry):
        arrived = copy(k, lax.rem(me + n - k, n))
        arrived.wait_send()
        arrived.wait_recv()
        return carry

    lax.fori_loop(1, n, start, 0)
    own = pltpu.make_async_copy(src, buf.at[me], own_sem)
    own.start()
    own.wait()
    lax.fori_loop(1, n, finish, 0)


def update_kernel(
    kept_part, cand_part, kept_ref, score_ref,
    kept_buf, cand_buf, send_sems, recv_sems,
    norm_buf, mine, line, plane, own_sem, line_send, line_recv, plane_send, plane_recv,
):
    nt, nb = lax.axis_size("tok"), lax.axis_size("blk")
    t, b = lax.axis_index("tok"), lax.axis_index("blk")
    kshare, cshare = kept_buf.shape[2], cand_buf.shape[2]
    blocks = kshare + cshare
    up_hops = nt // 2
    down_hops = nt - 1 - up_hops
    hops = (up_hops, down_hops)
    peers = (lax.rem(t + 1, nt), lax.rem(t + nt - 1, nt))

    barrier = pltpu.get_barrier_semaphore()
    greet(barrier, "tok", t, nt)
    greet(barrier, "blk", b, nb)

    def product(d, j):
        if j < kshare:
            return kept_part[d * kshare + j]
        return cand_part[d * cshare + (j - kshare)].astype(jnp.float32)

    def home(way, step):
        if way == 0:
            return lax.rem(t + up_hops - step + nt, nt)
        return lax.rem(t + nt - down_hops + step, nt)

    def block(way, step, j):
        if j < kshare:
            return kept_buf.at[way, step, j]
        return cand_buf.at[way, step, j - kshare]

    def copy(way, step, j):
        return pltpu.make_async_remote_copy(
            src_ref=block(way, step, j),
            dst_ref=block(way, step + 1, j),
            send_sem=send_sems.at[way, step, j],
            recv_sem=recv_sems.at[way, step, j],
            device_id={"tok": peers[way]},
            device_id_type=MESH,
        )

    def advance(way, step, j):
        term = product(home(way, step), j)
        copy(way, step - 1, j).wait_recv()
        here = block(way, step, j)
        here[...] = (here[...].astype(jnp.float32) + term).astype(here.dtype)
        copy(way, step, j).start()

    for way in range(2):
        for j in range(blocks):
            here = block(way, 0, j)
            here[...] = product(home(way, 0), j).astype(here.dtype)
    pl.semaphore_wait(barrier, nt + nb - 2)
    for j in range(blocks):
        for way in range(2):
            copy(way, 0, j).start()

    def both(step, carry):
        for j in range(blocks):
            for way in range(2):
                advance(way, step, j)
        return carry

    lax.fori_loop(1, down_hops, both, 0)
    for step in range(down_hops, up_hops):
        for j in range(blocks):
            advance(0, step, j)

    lane = lax.broadcasted_iota(jnp.int32, norm_buf.shape, 1)
    squares = jnp.zeros(norm_buf.shape, jnp.float32)
    for j in range(blocks):
        total = product(t, j)
        for way in (1, 0):
            copy(way, hops[way] - 1, j).wait_recv()
            total = total + block(way, hops[way], j)[...].astype(jnp.float32)
        if j < kshare:
            kept_ref[j] = total.astype(kept_ref.dtype)
        else:
            squares = jnp.where(lane == j - kshare, jnp.sum(total * total), squares)
    norms = jnp.sqrt(squares)
    norm_buf[...] = norms
    own = pltpu.make_async_copy(norm_buf, mine, own_sem)
    own.start()

    def sent(step, carry):
        for way in range(2):
            for j in range(blocks):
                copy(way, step, j).wait_send()
        return carry

    lax.fori_loop(0, down_hops, sent, 0)
    for step in range(down_hops, up_hops):
        for j in range(blocks):
            copy(0, step, j).wait_send()
    own.wait()

    exchange("tok", t, nt, mine, line, line_send, line_recv, own_sem)
    exchange("blk", b, nb, line, plane, plane_send, plane_recv, own_sem)
    score_ref[...] = norms / (jnp.max(plane[...]) + 1e-06)


def local(acts, out_grad, kept_ids, cand_ids):
    owners = lax.axis_size("blk")
    owner_index = lax.axis_index("blk")
    ncols = out_grad.shape[1] // BLOCK
    width = 2 * ((ncols + owners - 1) // owners)
    tokens = acts.shape[0]
    per = acts.shape[1] // BLOCK
    slot_ids = jnp.concatenate([kept_ids, cand_ids], axis=1)
    acts_all = lax.all_gather(acts, "blk", axis=0, tiled=False)
    table, position = column_tables(slot_ids % ncols, width)
    vmem = pl.BlockSpec(memory_space=pltpu.VMEM)
    smem = pl.BlockSpec(memory_space=pltpu.SMEM)
    outgoing = pl.pallas_call(
        lambda *refs: pick_kernel(owners, width, *refs),
        out_shape=jax.ShapeDtypeStruct((owners, out_grad.shape[0], width * BLOCK), out_grad.dtype),
        in_specs=[smem, vmem],
        out_specs=vmem,
        name="pick",
    )(table.reshape(-1), out_grad)
    incoming = lax.all_to_all(outgoing, "blk", split_axis=0, concat_axis=0, tiled=True)
    grad_cols = incoming.reshape(tokens, width * BLOCK)
    my_rows = lax.dynamic_index_in_dim(slot_ids // ncols, owner_index, 0, keepdims=False)
    my_cols = lax.dynamic_index_in_dim(position, owner_index, 0, keepdims=False)
    kept_part, cand_part = pl.pallas_call(
        lambda *refs: product_kernel(per, *refs),
        out_shape=(
            jax.ShapeDtypeStruct((KS, BLOCK, BLOCK), jnp.float32),
            jax.ShapeDtypeStruct((cand_ids.shape[1], BLOCK, BLOCK), jnp.bfloat16),
        ),
        in_specs=[smem, smem, vmem, vmem],
        out_specs=(vmem, vmem),
        name="products",
    )(my_rows, my_cols, acts_all, grad_cols)
    toks = lax.axis_size("tok")
    kshare, share = KS // toks, cand_ids.shape[1] // toks
    steps = toks // 2
    dma = pltpu.SemaphoreType.DMA
    kept_grad, scores = pl.pallas_call(
        update_kernel,
        out_shape=(
            jax.ShapeDtypeStruct((kshare, BLOCK, BLOCK), jnp.bfloat16),
            jax.ShapeDtypeStruct((1, BLOCK), jnp.float32),
        ),
        in_specs=[vmem, vmem],
        out_specs=(vmem, vmem),
        scratch_shapes=[
            pltpu.VMEM((2, steps + 1, kshare, BLOCK, BLOCK), jnp.float32),
            pltpu.VMEM((2, steps + 1, share, BLOCK, BLOCK), jnp.bfloat16),
            dma((2, steps, kshare + share)),
            dma((2, steps, kshare + share)),
            pltpu.VMEM((1, BLOCK), jnp.float32),
            pltpu.VMEM((1, BLOCK), jnp.float32),
            pltpu.VMEM((toks, 1, BLOCK), jnp.float32),
            pltpu.VMEM((owners, toks, 1, BLOCK), jnp.float32),
            dma,
            dma((toks,)),
            dma((toks,)),
            dma((owners,)),
            dma((owners,)),
        ],
        compiler_params=pltpu.CompilerParams(collective_id=0, has_side_effects=True),
        name="update",
    )(kept_part, cand_part)
    cand_score = scores[:, :share]
    return (kept_grad[None], cand_score)


def solution(mesh):
    return jax.shard_map(
        local,
        mesh=mesh,
        in_specs=(P("tok", "blk"), P(("tok", "blk"), None), P(), P()),
        out_specs=(P("blk", "tok", None, None), P("blk", "tok")),
        check_vma=False,
    )
```

```python
import jax
import jax.numpy as jnp
from jax import lax
from jax.experimental import pallas as pl
from jax.experimental.pallas import tpu as pltpu
from jax.sharding import PartitionSpec as P

BLOCK = 128
KS = 16


def column_tables(cols, width):
    slots = cols.shape[1]
    same = cols[:, :, None] == cols[:, None, :]
    place = jnp.arange(slots)
    earlier = place[None, :] < place[:, None]
    first = jnp.logical_not(jnp.any(same & earlier[None], axis=2))
    rank = jnp.sum(jnp.where(earlier[None] & first[:, None, :], 1, 0), axis=2)
    position = jnp.sum(jnp.where(same & first[:, None, :], rank[:, None, :], 0), axis=2)
    hit = first[:, None, :] & (rank[:, None, :] == jnp.arange(width)[None, :, None])
    table = jnp.sum(jnp.where(hit, cols[:, None, :], 0), axis=2)
    return table.astype(jnp.int32), position.astype(jnp.int32)


def pick_kernel(owners, width, table_ref, grad_ref, out_ref):
    def one_owner(o, carry):
        for w in range(width):
            col = table_ref[o * width + w]
            out_ref[o, :, w * BLOCK : (w + 1) * BLOCK] = grad_ref[
                :, pl.ds(pl.multiple_of(col * BLOCK, BLOCK), BLOCK)
            ]
        return carry

    lax.fori_loop(0, owners, one_owner, 0)


def product_kernel(per, rows_ref, cols_ref, acts_ref, grad_ref, kept_ref, cand_ref):
    def product(slot):
        row = rows_ref[slot]
        col = cols_ref[slot]
        left = acts_ref[row // per, :, pl.ds(pl.multiple_of((row % per) * BLOCK, BLOCK), BLOCK)]
        right = grad_ref[:, pl.ds(pl.multiple_of(col * BLOCK, BLOCK), BLOCK)]
        return lax.dot_general(
            left, right, (((0,), (0,)), ((), ())), preferred_element_type=jnp.float32
        )

    def kept(j, carry):
        for u in range(4):
            kept_ref[4 * j + u] = product(4 * j + u)
        return carry

    def cand(j, carry):
        for u in range(4):
            cand_ref[4 * j + u] = product(kept_ref.shape[0] + 4 * j + u).astype(cand_ref.dtype)
        return carry

    lax.fori_loop(0, kept_ref.shape[0] // 4, kept, 0)
    lax.fori_loop(0, cand_ref.shape[0] // 4, cand, 0)


MESH = pl.DeviceIdType.MESH


def greet(barrier, axis, me, n):
    def one(k, carry):
        pl.semaphore_signal(
            barrier, inc=1, device_id={axis: lax.rem(me + k, n)}, device_id_type=MESH
        )
        return carry

    lax.fori_loop(1, n, one, 0)


def exchange(axis, me, n, src, buf, send, recv, own_sem):
    def copy(k, slot):
        return pltpu.make_async_remote_copy(
            src_ref=src,
            dst_ref=buf.at[slot],
            send_sem=send.at[k],
            recv_sem=recv.at[k],
            device_id={axis: lax.rem(me + k, n)},
            device_id_type=MESH,
        )

    def start(k, carry):
        copy(k, me).start()
        return carry

    def finish(k, carry):
        arrived = copy(k, lax.rem(me + n - k, n))
        arrived.wait_send()
        arrived.wait_recv()
        return carry

    lax.fori_loop(1, n, start, 0)
    own = pltpu.make_async_copy(src, buf.at[me], own_sem)
    own.start()
    own.wait()
    lax.fori_loop(1, n, finish, 0)


def gather_kernel(
    acts_ref, out_ref, all_ref, in_ref,
    own_sem, acts_send, acts_recv, relay_send, relay_recv, grad_send, grad_recv,
):
    nb = lax.axis_size("blk")
    b = lax.axis_index("blk")
    partner = b + 1 - 2 * lax.rem(b, 2)
    chips = nb // 2
    barrier = pltpu.get_barrier_semaphore()
    greet(barrier, "blk", b, nb)
    pl.semaphore_wait(barrier, nb - 1)

    def remote(src, dst, send, recv, peer):
        return pltpu.make_async_remote_copy(
            src_ref=src,
            dst_ref=dst,
            send_sem=send,
            recv_sem=recv,
            device_id={"blk": peer},
            device_id_type=MESH,
        )

    def acts_copy(k, slot):
        return remote(
            acts_ref, all_ref.at[slot], acts_send.at[k], acts_recv.at[k], lax.rem(b + 2 * k, nb)
        )

    def relay_copy(k, slot):
        return remote(
            all_ref.at[slot], all_ref.at[slot], relay_send.at[k], relay_recv.at[k], partner
        )

    def grad_copy(k, slot):
        peer = lax.rem(b + k, nb)
        return remote(out_ref.at[peer], in_ref.at[slot], grad_send.at[k], grad_recv.at[k], peer)

    def start_acts(k, carry):
        acts_copy(k, b).start()
        return carry

    def start_grad(k, carry):
        grad_copy(k, b).start()
        return carry

    own_relay = remote(acts_ref, all_ref.at[b], relay_send.at[0], relay_recv.at[0], partner)
    lax.fori_loop(1, chips, start_acts, 0)
    own_relay.start()
    lax.fori_loop(1, nb, start_grad, 0)
    own_acts = pltpu.make_async_copy(acts_ref, all_ref.at[b], own_sem.at[0])
    own_grad = pltpu.make_async_copy(out_ref.at[b], in_ref.at[b], own_sem.at[1])
    own_acts.start()
    own_grad.start()

    def relay(k, carry):
        slot = lax.rem(b + nb - 2 * k, nb)
        acts_copy(k, slot).wait_recv()
        relay_copy(k, slot).start()
        return carry

    lax.fori_loop(1, chips, relay, 0)

    def finish_grad(k, carry):
        arrived = grad_copy(k, lax.rem(b + nb - k, nb))
        arrived.wait_send()
        arrived.wait_recv()
        return carry

    def finish_acts(k, carry):
        acts_copy(k, b).wait_send()
        slot = lax.rem(partner + nb - 2 * k, nb)
        relay_copy(k, slot).wait_send()
        relay_copy(k, slot).wait_recv()
        return carry

    lax.fori_loop(1, nb, finish_grad, 0)
    own_relay.wait_send()
    remote(acts_ref, all_ref.at[partner], relay_send.at[0], relay_recv.at[0], partner).wait_recv()
    lax.fori_loop(1, chips, finish_acts, 0)
    own_acts.wait()
    own_grad.wait()


def update_kernel(
    kept_part, cand_part, kept_ref, score_ref,
    kept_buf, cand_buf, send_sems, recv_sems,
    norm_buf, mine, line, plane, own_sem, line_send, line_recv, plane_send, plane_recv,
):
    nt, nb = lax.axis_size("tok"), lax.axis_size("blk")
    t, b = lax.axis_index("tok"), lax.axis_index("blk")
    kshare, cshare = kept_buf.shape[2], cand_buf.shape[2]
    blocks = kshare + cshare
    up_hops = nt // 2
    down_hops = nt - 1 - up_hops
    hops = (up_hops, down_hops)
    peers = (lax.rem(t + 1, nt), lax.rem(t + nt - 1, nt))

    barrier = pltpu.get_barrier_semaphore()
    greet(barrier, "tok", t, nt)
    greet(barrier, "blk", b, nb)

    def product(d, j):
        if j < kshare:
            return kept_part[d * kshare + j]
        return cand_part[d * cshare + (j - kshare)].astype(jnp.float32)

    def home(way, step):
        if way == 0:
            return lax.rem(t + up_hops - step + nt, nt)
        return lax.rem(t + nt - down_hops + step, nt)

    def block(way, step, j):
        if j < kshare:
            return kept_buf.at[way, step, j]
        return cand_buf.at[way, step, j - kshare]

    def copy(way, step, j):
        return pltpu.make_async_remote_copy(
            src_ref=block(way, step, j),
            dst_ref=block(way, step + 1, j),
            send_sem=send_sems.at[way, step, j],
            recv_sem=recv_sems.at[way, step, j],
            device_id={"tok": peers[way]},
            device_id_type=MESH,
        )

    def advance(way, step, j):
        term = product(home(way, step), j)
        copy(way, step - 1, j).wait_recv()
        here = block(way, step, j)
        here[...] = (here[...].astype(jnp.float32) + term).astype(here.dtype)
        copy(way, step, j).start()

    for way in range(2):
        for j in range(blocks):
            here = block(way, 0, j)
            here[...] = product(home(way, 0), j).astype(here.dtype)
    pl.semaphore_wait(barrier, nt + nb - 2)
    for j in range(blocks):
        for way in range(2):
            copy(way, 0, j).start()

    def both(step, carry):
        for j in range(blocks):
            for way in range(2):
                advance(way, step, j)
        return carry

    lax.fori_loop(1, down_hops, both, 0)
    for step in range(down_hops, up_hops):
        for j in range(blocks):
            advance(0, step, j)

    lane = lax.broadcasted_iota(jnp.int32, norm_buf.shape, 1)
    squares = jnp.zeros(norm_buf.shape, jnp.float32)
    for j in range(blocks):
        total = product(t, j)
        for way in (1, 0):
            copy(way, hops[way] - 1, j).wait_recv()
            total = total + block(way, hops[way], j)[...].astype(jnp.float32)
        if j < kshare:
            kept_ref[j] = total.astype(kept_ref.dtype)
        else:
            squares = jnp.where(lane == j - kshare, jnp.sum(total * total), squares)
    norms = jnp.sqrt(squares)
    norm_buf[...] = norms
    own = pltpu.make_async_copy(norm_buf, mine, own_sem)
    own.start()

    def sent(step, carry):
        for way in range(2):
            for j in range(blocks):
                copy(way, step, j).wait_send()
        return carry

    lax.fori_loop(0, down_hops, sent, 0)
    for step in range(down_hops, up_hops):
        for j in range(blocks):
            copy(0, step, j).wait_send()
    own.wait()

    exchange("tok", t, nt, mine, line, line_send, line_recv, own_sem)
    exchange("blk", b, nb, line, plane, plane_send, plane_recv, own_sem)
    score_ref[...] = norms / (jnp.max(plane[...]) + 1e-06)


def local(acts, out_grad, kept_ids, cand_ids):
    owners = lax.axis_size("blk")
    owner_index = lax.axis_index("blk")
    ncols = out_grad.shape[1] // BLOCK
    width = 2 * ((ncols + owners - 1) // owners)
    tokens = acts.shape[0]
    per = acts.shape[1] // BLOCK
    slot_ids = jnp.concatenate([kept_ids, cand_ids], axis=1)
    table, position = column_tables(slot_ids % ncols, width)
    vmem = pl.BlockSpec(memory_space=pltpu.VMEM)
    smem = pl.BlockSpec(memory_space=pltpu.SMEM)
    outgoing = pl.pallas_call(
        lambda *refs: pick_kernel(owners, width, *refs),
        out_shape=jax.ShapeDtypeStruct((owners, out_grad.shape[0], width * BLOCK), out_grad.dtype),
        in_specs=[smem, vmem],
        out_specs=vmem,
        name="pick",
    )(table.reshape(-1), out_grad)
    dma = pltpu.SemaphoreType.DMA
    chips = owners // 2
    acts_all, incoming = pl.pallas_call(
        gather_kernel,
        out_shape=(
            jax.ShapeDtypeStruct((owners,) + acts.shape, acts.dtype),
            jax.ShapeDtypeStruct(outgoing.shape, outgoing.dtype),
        ),
        in_specs=[vmem, vmem],
        out_specs=(vmem, vmem),
        scratch_shapes=[
            dma((2,)),
            dma((chips,)),
            dma((chips,)),
            dma((chips,)),
            dma((chips,)),
            dma((owners,)),
            dma((owners,)),
        ],
        compiler_params=pltpu.CompilerParams(collective_id=1, has_side_effects=True),
        name="gather",
    )(acts, outgoing)
    grad_cols = incoming.reshape(tokens, width * BLOCK)
    my_rows = lax.dynamic_index_in_dim(slot_ids // ncols, owner_index, 0, keepdims=False)
    my_cols = lax.dynamic_index_in_dim(position, owner_index, 0, keepdims=False)
    kept_part, cand_part = pl.pallas_call(
        lambda *refs: product_kernel(per, *refs),
        out_shape=(
            jax.ShapeDtypeStruct((KS, BLOCK, BLOCK), jnp.float32),
            jax.ShapeDtypeStruct((cand_ids.shape[1], BLOCK, BLOCK), jnp.bfloat16),
        ),
        in_specs=[smem, smem, vmem, vmem],
        out_specs=(vmem, vmem),
        name="products",
    )(my_rows, my_cols, acts_all, grad_cols)
    toks = lax.axis_size("tok")
    kshare, share = KS // toks, cand_ids.shape[1] // toks
    steps = toks // 2
    kept_grad, scores = pl.pallas_call(
        update_kernel,
        out_shape=(
            jax.ShapeDtypeStruct((kshare, BLOCK, BLOCK), jnp.bfloat16),
            jax.ShapeDtypeStruct((1, BLOCK), jnp.float32),
        ),
        in_specs=[vmem, vmem],
        out_specs=(vmem, vmem),
        scratch_shapes=[
            pltpu.VMEM((2, steps + 1, kshare, BLOCK, BLOCK), jnp.float32),
            pltpu.VMEM((2, steps + 1, share, BLOCK, BLOCK), jnp.bfloat16),
            dma((2, steps, kshare + share)),
            dma((2, steps, kshare + share)),
            pltpu.VMEM((1, BLOCK), jnp.float32),
            pltpu.VMEM((1, BLOCK), jnp.float32),
            pltpu.VMEM((toks, 1, BLOCK), jnp.float32),
            pltpu.VMEM((owners, toks, 1, BLOCK), jnp.float32),
            dma,
            dma((toks,)),
            dma((toks,)),
            dma((owners,)),
            dma((owners,)),
        ],
        compiler_params=pltpu.CompilerParams(collective_id=0, has_side_effects=True),
        name="update",
    )(kept_part, cand_part)
    cand_score = scores[:, :share]
    return (kept_grad[None], cand_score)


def solution(mesh):
    return jax.shard_map(
        local,
        mesh=mesh,
        in_specs=(P("tok", "blk"), P(("tok", "blk"), None), P(), P()),
        out_specs=(P("blk", "tok", None, None), P("blk", "tok")),
        check_vma=False,
    )
```

```python
import math

import jax
import jax.numpy as jnp
from jax import lax
from jax.experimental import pallas as pl
from jax.experimental.pallas import tpu as pltpu
from jax.sharding import PartitionSpec as P

BLOCK = 128
KS = 16


def column_tables(cols, width):
    slots = cols.shape[1]
    same = cols[:, :, None] == cols[:, None, :]
    place = jnp.arange(slots)
    earlier = place[None, :] < place[:, None]
    first = jnp.logical_not(jnp.any(same & earlier[None], axis=2))
    rank = jnp.sum(jnp.where(earlier[None] & first[:, None, :], 1, 0), axis=2)
    position = jnp.sum(jnp.where(same & first[:, None, :], rank[:, None, :], 0), axis=2)
    hit = first[:, None, :] & (rank[:, None, :] == jnp.arange(width)[None, :, None])
    table = jnp.sum(jnp.where(hit, cols[:, None, :], 0), axis=2)
    return table.astype(jnp.int32), position.astype(jnp.int32)


def pick_kernel(owners, width, table_ref, grad_ref, out_ref):
    def one_owner(o, carry):
        for w in range(width):
            col = table_ref[o * width + w]
            out_ref[o, :, w * BLOCK : (w + 1) * BLOCK] = grad_ref[
                :, pl.ds(pl.multiple_of(col * BLOCK, BLOCK), BLOCK)
            ]
        return carry

    lax.fori_loop(0, owners, one_owner, 0)


MESH = pl.DeviceIdType.MESH


def greet(barrier, axis, me, n):
    def one(k, carry):
        pl.semaphore_signal(
            barrier, inc=1, device_id={axis: lax.rem(me + k, n)}, device_id_type=MESH
        )
        return carry

    lax.fori_loop(1, n, one, 0)


def exchange(axis, me, n, src, buf, send, recv, own_sem):
    def copy(k, slot):
        return pltpu.make_async_remote_copy(
            src_ref=src,
            dst_ref=buf.at[slot],
            send_sem=send.at[k],
            recv_sem=recv.at[k],
            device_id={axis: lax.rem(me + k, n)},
            device_id_type=MESH,
        )

    def start(k, carry):
        copy(k, me).start()
        return carry

    def finish(k, carry):
        arrived = copy(k, lax.rem(me + n - k, n))
        arrived.wait_send()
        arrived.wait_recv()
        return carry

    lax.fori_loop(1, n, start, 0)
    own = pltpu.make_async_copy(src, buf.at[me], own_sem)
    own.start()
    own.wait()
    lax.fori_loop(1, n, finish, 0)


def gather_kernel(
    acts_ref, out_ref, all_ref, in_ref,
    own_sem, acts_send, acts_recv, relay_send, relay_recv, grad_send, grad_recv,
):
    nb = lax.axis_size("blk")
    b = lax.axis_index("blk")
    partner = b + 1 - 2 * lax.rem(b, 2)
    side = acts_send.shape[1]
    barrier = pltpu.get_barrier_semaphore()
    greet(barrier, "blk", b, nb)
    pl.semaphore_wait(barrier, nb - 1)

    def remote(src, dst, send, recv, peer):
        return pltpu.make_async_remote_copy(
            src_ref=src,
            dst_ref=dst,
            send_sem=send,
            recv_sem=recv,
            device_id={"blk": peer},
            device_id_type=MESH,
        )

    core = lax.rem(b, 2)
    spot = (lax.rem(b // 2, side), b // (2 * side))
    halves = tuple(
        acts_ref.at[:, pl.ds(h * BLOCK, BLOCK)] for h in range(2)
    )

    def device(h, first, second):
        p = lax.rem(spot[h] + first + side, side)
        q = lax.rem(spot[1 - h] + second + side, side)
        x, y = (p, q) if h == 0 else (q, p)
        return (y * side + x) * 2 + core

    def held(h, i, j):
        return all_ref.at[device(h, -i, -j), h]

    def hop(h, i, j, step):
        i0, j0 = (i - step[0]) % side, (j - step[1]) % side
        here = halves[h] if i0 == 0 and j0 == 0 else held(h, i0, j0)
        return remote(
            here,
            held(h, i0, j0),
            acts_send.at[h, i, j],
            acts_recv.at[h, i, j],
            device(h, step[0], step[1]),
        )

    def landing(h, i, j):
        return remote(held(h, i, j), held(h, i, j), acts_send.at[h, i, j], acts_recv.at[h, i, j], partner)

    def relay_copy(h, i, j):
        here = halves[h] if i == 0 and j == 0 else held(h, i, j)
        return remote(here, held(h, i, j), relay_send.at[h, i, j], relay_recv.at[h, i, j], partner)

    def relay_landing(h, i, j):
        block = all_ref.at[device(h, -i, -j) + 1 - 2 * core, h]
        return remote(block, block, relay_send.at[h, i, j], relay_recv.at[h, i, j], partner)

    def forward(h, i, j):
        way = 1 if h == 0 else -1
        if j == 0:
            if i == 0:
                hop(h, 1, 0, (1, 0)).start()
                hop(h, side - 1, 0, (-1, 0)).start()
            elif i == way % side:
                hop(h, 2, 0, (way, 0)).start()
            hop(h, i, 1, (0, 1)).start()
            hop(h, i, side - 1, (0, -1)).start()
        elif j == way % side:
            hop(h, i, 2, (0, way)).start()
        relay_copy(h, i, j).start()

    def arrive(h, i, j):
        landing(h, i, j).wait_recv()
        forward(h, i, j)

    def grad_copy(k, slot):
        peer = lax.rem(b + k, nb)
        return remote(out_ref.at[peer], in_ref.at[slot], grad_send.at[k], grad_recv.at[k], peer)

    def start_grad(k, carry):
        grad_copy(k, b).start()
        return carry

    for h in range(2):
        forward(h, 0, 0)
    for i, j in ((1, 0), (3, 0), (0, 1), (0, 3)):
        for h in range(2):
            arrive(h, i, j)
    lax.fori_loop(1, nb, start_grad, 0)
    own_acts = [
        pltpu.make_async_copy(halves[h], all_ref.at[b, h], own_sem.at[h]) for h in range(2)
    ]
    own_grad = pltpu.make_async_copy(out_ref.at[b], in_ref.at[b], own_sem.at[2])
    for own in (*own_acts, own_grad):
        own.start()
    later = ((2, 0), (0, 2), (1, 1), (1, 3), (3, 1), (3, 3), (1, 2), (3, 2), (2, 1), (2, 3), (2, 2))
    for i, j in later:
        for h in range(2):
            arrive(h, i, j)

    def finish_grad(k, carry):
        arrived = grad_copy(k, lax.rem(b + nb - k, nb))
        arrived.wait_send()
        arrived.wait_recv()
        return carry

    lax.fori_loop(1, nb, finish_grad, 0)
    for h in range(2):
        for i in range(side):
            for j in range(side):
                if i or j:
                    landing(h, i, j).wait_send()
                relay_landing(h, i, j).wait_send()
                relay_landing(h, i, j).wait_recv()
    for own in (*own_acts, own_grad):
        own.wait()


def update_kernel(
    row_ref, col_ref, acts_ref, grad_ref, kept_ref, score_ref,
    cols, kept_buf, cand_buf, send_sems, recv_sems,
    norm_buf, mine, line, plane, own_sem, line_send, line_recv, plane_send, plane_recv,
):
    nt, nb = lax.axis_size("tok"), lax.axis_size("blk")
    t, b = lax.axis_index("tok"), lax.axis_index("blk")
    kshare, cshare = kept_buf.shape[2], cand_buf.shape[2]
    blocks = kshare + cshare
    up_hops = nt // 2
    down_hops = nt - 1 - up_hops
    hops = (up_hops, down_hops)
    peers = (lax.rem(t + 1, nt), lax.rem(t + nt - 1, nt))

    barrier = pltpu.get_barrier_semaphore()
    greet(barrier, "tok", t, nt)
    greet(barrier, "blk", b, nb)

    for w in range(cols.shape[0]):
        cols[w] = grad_ref[:, w * BLOCK : (w + 1) * BLOCK]

    def product(d, j):
        slot = d * kshare + j if j < kshare else nt * kshare + d * cshare + (j - kshare)
        left = acts_ref[row_ref[slot]]
        right = cols[col_ref[slot]]
        return lax.dot_general(
            left, right, (((0,), (0,)), ((), ())), preferred_element_type=jnp.float32
        )

    def home(way, step):
        if way == 0:
            return lax.rem(t + up_hops - step + nt, nt)
        return lax.rem(t + nt - down_hops + step, nt)

    def block(way, step, j):
        if j < kshare:
            return kept_buf.at[way, step, j]
        return cand_buf.at[way, step, j - kshare]

    def copy(way, step, j):
        return pltpu.make_async_remote_copy(
            src_ref=block(way, step, j),
            dst_ref=block(way, step + 1, j),
            send_sem=send_sems.at[way, step, j],
            recv_sem=recv_sems.at[way, step, j],
            device_id={"tok": peers[way]},
            device_id_type=MESH,
        )

    def advance(way, step, j):
        term = product(home(way, step), j)
        copy(way, step - 1, j).wait_recv()
        here = block(way, step, j)
        here[...] = (here[...].astype(jnp.float32) + term).astype(here.dtype)
        copy(way, step, j).start()

    for way in range(2):
        for j in range(blocks):
            here = block(way, 0, j)
            here[...] = product(home(way, 0), j).astype(here.dtype)
    pl.semaphore_wait(barrier, nt + nb - 2)
    for j in range(blocks):
        for way in range(2):
            copy(way, 0, j).start()

    def both(step, carry):
        for j in range(blocks):
            for way in range(2):
                advance(way, step, j)
        return carry

    lax.fori_loop(1, down_hops, both, 0)
    for step in range(down_hops, up_hops):
        for j in range(blocks):
            advance(0, step, j)

    lane = lax.broadcasted_iota(jnp.int32, norm_buf.shape, 1)
    squares = jnp.zeros(norm_buf.shape, jnp.float32)
    for j in range(blocks):
        total = product(t, j)
        for way in (1, 0):
            copy(way, hops[way] - 1, j).wait_recv()
            total = total + block(way, hops[way], j)[...].astype(jnp.float32)
        if j < kshare:
            kept_ref[j] = total.astype(kept_ref.dtype)
        else:
            squares = jnp.where(lane == j - kshare, jnp.sum(total * total), squares)
    norms = jnp.sqrt(squares)
    norm_buf[...] = norms
    own = pltpu.make_async_copy(norm_buf, mine, own_sem)
    own.start()

    def sent(step, carry):
        for way in range(2):
            for j in range(blocks):
                copy(way, step, j).wait_send()
        return carry

    lax.fori_loop(0, down_hops, sent, 0)
    for step in range(down_hops, up_hops):
        for j in range(blocks):
            copy(0, step, j).wait_send()
    own.wait()

    exchange("tok", t, nt, mine, line, line_send, line_recv, own_sem)
    exchange("blk", b, nb, line, plane, plane_send, plane_recv, own_sem)
    score_ref[...] = norms / (jnp.max(plane[...]) + 1e-06)


def local(acts, out_grad, kept_ids, cand_ids):
    owners = lax.axis_size("blk")
    owner_index = lax.axis_index("blk")
    ncols = out_grad.shape[1] // BLOCK
    width = 2 * ((ncols + owners - 1) // owners)
    tokens = acts.shape[0]
    per = acts.shape[1] // BLOCK
    slot_ids = jnp.concatenate([kept_ids, cand_ids], axis=1)
    table, position = column_tables(slot_ids % ncols, width)
    vmem = pl.BlockSpec(memory_space=pltpu.VMEM)
    smem = pl.BlockSpec(memory_space=pltpu.SMEM)
    outgoing = pl.pallas_call(
        lambda *refs: pick_kernel(owners, width, *refs),
        out_shape=jax.ShapeDtypeStruct((owners, out_grad.shape[0], width * BLOCK), out_grad.dtype),
        in_specs=[smem, vmem],
        out_specs=vmem,
        name="pick",
    )(table.reshape(-1), out_grad)
    dma = pltpu.SemaphoreType.DMA
    side = math.isqrt(owners // 2)
    acts_all, incoming = pl.pallas_call(
        gather_kernel,
        out_shape=(
            jax.ShapeDtypeStruct((owners, per, tokens, BLOCK), acts.dtype),
            jax.ShapeDtypeStruct(outgoing.shape, outgoing.dtype),
        ),
        in_specs=[vmem, vmem],
        out_specs=(vmem, vmem),
        scratch_shapes=[
            dma((3,)),
            dma((per, side, side)),
            dma((per, side, side)),
            dma((per, side, side)),
            dma((per, side, side)),
            dma((owners,)),
            dma((owners,)),
        ],
        compiler_params=pltpu.CompilerParams(collective_id=1, has_side_effects=True),
        name="gather",
    )(acts, outgoing)
    acts_all = acts_all.reshape(owners * per, tokens, BLOCK)
    grad_cols = incoming.reshape(tokens, width * BLOCK)
    my_rows = lax.dynamic_index_in_dim(slot_ids // ncols, owner_index, 0, keepdims=False)
    my_cols = lax.dynamic_index_in_dim(position, owner_index, 0, keepdims=False)
    toks = lax.axis_size("tok")
    kshare, share = KS // toks, cand_ids.shape[1] // toks
    steps = toks // 2
    kept_grad, scores = pl.pallas_call(
        update_kernel,
        out_shape=(
            jax.ShapeDtypeStruct((kshare, BLOCK, BLOCK), jnp.bfloat16),
            jax.ShapeDtypeStruct((1, BLOCK), jnp.float32),
        ),
        in_specs=[smem, smem, vmem, vmem],
        out_specs=(vmem, vmem),
        scratch_shapes=[
            pltpu.VMEM((width, tokens, BLOCK), grad_cols.dtype),
            pltpu.VMEM((2, steps + 1, kshare, BLOCK, BLOCK), jnp.float32),
            pltpu.VMEM((2, steps + 1, share, BLOCK, BLOCK), jnp.bfloat16),
            dma((2, steps, kshare + share)),
            dma((2, steps, kshare + share)),
            pltpu.VMEM((1, BLOCK), jnp.float32),
            pltpu.VMEM((1, BLOCK), jnp.float32),
            pltpu.VMEM((toks, 1, BLOCK), jnp.float32),
            pltpu.VMEM((owners, toks, 1, BLOCK), jnp.float32),
            dma,
            dma((toks,)),
            dma((toks,)),
            dma((owners,)),
            dma((owners,)),
        ],
        compiler_params=pltpu.CompilerParams(collective_id=0, has_side_effects=True),
        name="update",
    )(my_rows, my_cols, acts_all, grad_cols)
    cand_score = scores[:, :share]
    return (kept_grad[None], cand_score)


def solution(mesh):
    return jax.shard_map(
        local,
        mesh=mesh,
        in_specs=(P("tok", "blk"), P(("tok", "blk"), None), P(), P()),
        out_specs=(P("blk", "tok", None, None), P("blk", "tok")),
        check_vma=False,
    )
```

```python
import math

import jax
import jax.numpy as jnp
from jax import lax
from jax.experimental import pallas as pl
from jax.experimental.pallas import tpu as pltpu
from jax.sharding import PartitionSpec as P

BLOCK = 128
KS = 16


def column_tables(cols, width):
    slots = cols.shape[1]
    same = cols[:, :, None] == cols[:, None, :]
    place = jnp.arange(slots)
    earlier = place[None, :] < place[:, None]
    first = jnp.logical_not(jnp.any(same & earlier[None], axis=2))
    rank = jnp.sum(jnp.where(earlier[None] & first[:, None, :], 1, 0), axis=2)
    position = jnp.sum(jnp.where(same & first[:, None, :], rank[:, None, :], 0), axis=2)
    hit = first[:, None, :] & (rank[:, None, :] == jnp.arange(width)[None, :, None])
    table = jnp.sum(jnp.where(hit, cols[:, None, :], 0), axis=2)
    return table.astype(jnp.int32), position.astype(jnp.int32)


def pick_kernel(owners, width, table_ref, grad_ref, out_ref):
    def one_owner(o, carry):
        for w in range(width):
            col = table_ref[o * width + w]
            out_ref[o, :, w * BLOCK : (w + 1) * BLOCK] = grad_ref[
                :, pl.ds(pl.multiple_of(col * BLOCK, BLOCK), BLOCK)
            ]
        return carry

    lax.fori_loop(0, owners, one_owner, 0)


MESH = pl.DeviceIdType.MESH


def greet(barrier, axis, me, n):
    def one(k, carry):
        pl.semaphore_signal(
            barrier, inc=1, device_id={axis: lax.rem(me + k, n)}, device_id_type=MESH
        )
        return carry

    lax.fori_loop(1, n, one, 0)


def exchange(axis, me, n, src, buf, send, recv, own_sem):
    def copy(k, slot):
        return pltpu.make_async_remote_copy(
            src_ref=src,
            dst_ref=buf.at[slot],
            send_sem=send.at[k],
            recv_sem=recv.at[k],
            device_id={axis: lax.rem(me + k, n)},
            device_id_type=MESH,
        )

    def start(k, carry):
        copy(k, me).start()
        return carry

    def finish(k, carry):
        arrived = copy(k, lax.rem(me + n - k, n))
        arrived.wait_send()
        arrived.wait_recv()
        return carry

    lax.fori_loop(1, n, start, 0)
    own = pltpu.make_async_copy(src, buf.at[me], own_sem)
    own.start()
    own.wait()
    lax.fori_loop(1, n, finish, 0)


def gather(
    acts_ref, out_ref, all_ref, in_ref,
    own_sem, acts_send, acts_recv, relay_send, relay_recv, grad_send, grad_recv,
):
    nb = lax.axis_size("blk")
    b = lax.axis_index("blk")
    partner = b + 1 - 2 * lax.rem(b, 2)
    side = acts_send.shape[1]
    per = acts_send.shape[0]

    def remote(src, dst, send, recv, peer):
        return pltpu.make_async_remote_copy(
            src_ref=src,
            dst_ref=dst,
            send_sem=send,
            recv_sem=recv,
            device_id={"blk": peer},
            device_id_type=MESH,
        )

    core = lax.rem(b, 2)
    spot = (lax.rem(b // 2, side), b // (2 * side))
    halves = tuple(
        acts_ref.at[:, pl.ds(h * BLOCK, BLOCK)] for h in range(2)
    )

    def device(h, first, second):
        p = lax.rem(spot[h] + first + side, side)
        q = lax.rem(spot[1 - h] + second + side, side)
        x, y = (p, q) if h == 0 else (q, p)
        return (y * side + x) * 2 + core

    def held(h, i, j):
        return all_ref.at[device(h, -i, -j) * per + h]

    def hop(h, i, j, step):
        i0, j0 = (i - step[0]) % side, (j - step[1]) % side
        here = halves[h] if i0 == 0 and j0 == 0 else held(h, i0, j0)
        return remote(
            here,
            held(h, i0, j0),
            acts_send.at[h, i, j],
            acts_recv.at[h, i, j],
            device(h, step[0], step[1]),
        )

    def landing(h, i, j):
        return remote(held(h, i, j), held(h, i, j), acts_send.at[h, i, j], acts_recv.at[h, i, j], partner)

    def relay_copy(h, i, j):
        here = halves[h] if i == 0 and j == 0 else held(h, i, j)
        return remote(here, held(h, i, j), relay_send.at[h, i, j], relay_recv.at[h, i, j], partner)

    def relay_landing(h, i, j):
        block = all_ref.at[(device(h, -i, -j) + 1 - 2 * core) * per + h]
        return remote(block, block, relay_send.at[h, i, j], relay_recv.at[h, i, j], partner)

    def forward(h, i, j):
        way = 1 if h == 0 else -1
        if j == 0:
            if i == 0:
                hop(h, 1, 0, (1, 0)).start()
                hop(h, side - 1, 0, (-1, 0)).start()
            elif i == way % side:
                hop(h, 2, 0, (way, 0)).start()
            hop(h, i, 1, (0, 1)).start()
            hop(h, i, side - 1, (0, -1)).start()
        elif j == way % side:
            hop(h, i, 2, (0, way)).start()
        relay_copy(h, i, j).start()

    def arrive(h, i, j):
        landing(h, i, j).wait_recv()
        forward(h, i, j)

    def grad_copy(k, slot):
        peer = lax.rem(b + k, nb)
        return remote(out_ref.at[peer], in_ref.at[slot], grad_send.at[k], grad_recv.at[k], peer)

    def start_grad(k, carry):
        grad_copy(k, b).start()
        return carry

    for h in range(2):
        forward(h, 0, 0)
    for i, j in ((1, 0), (3, 0), (0, 1), (0, 3)):
        for h in range(2):
            arrive(h, i, j)
    lax.fori_loop(1, nb, start_grad, 0)
    own_acts = [
        pltpu.make_async_copy(halves[h], all_ref.at[b * per + h], own_sem.at[h]) for h in range(2)
    ]
    own_grad = pltpu.make_async_copy(out_ref.at[b], in_ref.at[b], own_sem.at[2])
    for own in (*own_acts, own_grad):
        own.start()
    later = ((2, 0), (0, 2), (1, 1), (1, 3), (3, 1), (3, 3), (1, 2), (3, 2), (2, 1), (2, 3), (2, 2))
    for i, j in later:
        for h in range(2):
            arrive(h, i, j)

    def finish_grad(k, carry):
        arrived = grad_copy(k, lax.rem(b + nb - k, nb))
        arrived.wait_send()
        arrived.wait_recv()
        return carry

    lax.fori_loop(1, nb, finish_grad, 0)
    for h in range(2):
        for i in range(side):
            for j in range(side):
                if i or j:
                    landing(h, i, j).wait_send()
                relay_landing(h, i, j).wait_send()
                relay_landing(h, i, j).wait_recv()
    for own in (*own_acts, own_grad):
        own.wait()


def update_kernel(
    row_ref, col_ref, acts_ref, out_ref, kept_ref, score_ref,
    all_ref, in_ref, gather_own, acts_send, acts_recv, relay_send, relay_recv, grad_send, grad_recv,
    cols, kept_buf, cand_buf, send_sems, recv_sems,
    norm_buf, mine, line, plane, own_sem, line_send, line_recv, plane_send, plane_recv,
):
    nt, nb = lax.axis_size("tok"), lax.axis_size("blk")
    t, b = lax.axis_index("tok"), lax.axis_index("blk")
    kshare, cshare = kept_buf.shape[2], cand_buf.shape[2]
    blocks = kshare + cshare
    up_hops = nt // 2
    down_hops = nt - 1 - up_hops
    hops = (up_hops, down_hops)
    peers = (lax.rem(t + 1, nt), lax.rem(t + nt - 1, nt))

    barrier = pltpu.get_barrier_semaphore()
    greet(barrier, "tok", t, nt)
    greet(barrier, "blk", b, nb)
    pl.semaphore_wait(barrier, nt + nb - 2)
    gather(
        acts_ref, out_ref, all_ref, in_ref,
        gather_own, acts_send, acts_recv, relay_send, relay_recv, grad_send, grad_recv,
    )
    for w in range(cols.shape[0]):
        rows = in_ref[:, :, w * BLOCK : (w + 1) * BLOCK].astype(jnp.float32)
        cols[w] = rows.reshape(cols.shape[1:]).astype(cols.dtype)

    def product(d, j):
        slot = d * kshare + j if j < kshare else nt * kshare + d * cshare + (j - kshare)
        left = all_ref[row_ref[slot]]
        right = cols[col_ref[slot]]
        return lax.dot_general(
            left, right, (((0,), (0,)), ((), ())), preferred_element_type=jnp.float32
        )

    def home(way, step):
        if way == 0:
            return lax.rem(t + up_hops - step + nt, nt)
        return lax.rem(t + nt - down_hops + step, nt)

    def block(way, step, j):
        if j < kshare:
            return kept_buf.at[way, step, j]
        return cand_buf.at[way, step, j - kshare]

    def copy(way, step, j):
        return pltpu.make_async_remote_copy(
            src_ref=block(way, step, j),
            dst_ref=block(way, step + 1, j),
            send_sem=send_sems.at[way, step, j],
            recv_sem=recv_sems.at[way, step, j],
            device_id={"tok": peers[way]},
            device_id_type=MESH,
        )

    def advance(way, step, j):
        term = product(home(way, step), j)
        copy(way, step - 1, j).wait_recv()
        here = block(way, step, j)
        here[...] = (here[...].astype(jnp.float32) + term).astype(here.dtype)
        copy(way, step, j).start()

    for way in range(2):
        for j in range(blocks):
            here = block(way, 0, j)
            here[...] = product(home(way, 0), j).astype(here.dtype)
    for j in range(blocks):
        for way in range(2):
            copy(way, 0, j).start()

    def both(step, carry):
        for j in range(blocks):
            for way in range(2):
                advance(way, step, j)
        return carry

    lax.fori_loop(1, down_hops, both, 0)
    for step in range(down_hops, up_hops):
        for j in range(blocks):
            advance(0, step, j)

    lane = lax.broadcasted_iota(jnp.int32, norm_buf.shape, 1)
    squares = jnp.zeros(norm_buf.shape, jnp.float32)
    for j in range(blocks):
        total = product(t, j)
        for way in (1, 0):
            copy(way, hops[way] - 1, j).wait_recv()
            total = total + block(way, hops[way], j)[...].astype(jnp.float32)
        if j < kshare:
            kept_ref[j] = total.astype(kept_ref.dtype)
        else:
            squares = jnp.where(lane == j - kshare, jnp.sum(total * total), squares)
    norms = jnp.sqrt(squares)
    norm_buf[...] = norms
    own = pltpu.make_async_copy(norm_buf, mine, own_sem)
    own.start()

    def sent(step, carry):
        for way in range(2):
            for j in range(blocks):
                copy(way, step, j).wait_send()
        return carry

    lax.fori_loop(0, down_hops, sent, 0)
    for step in range(down_hops, up_hops):
        for j in range(blocks):
            copy(0, step, j).wait_send()
    own.wait()

    exchange("tok", t, nt, mine, line, line_send, line_recv, own_sem)
    exchange("blk", b, nb, line, plane, plane_send, plane_recv, own_sem)
    score_ref[...] = norms / (jnp.max(plane[...]) + 1e-06)


def local(acts, out_grad, kept_ids, cand_ids):
    owners = lax.axis_size("blk")
    owner_index = lax.axis_index("blk")
    ncols = out_grad.shape[1] // BLOCK
    width = 2 * ((ncols + owners - 1) // owners)
    tokens = acts.shape[0]
    per = acts.shape[1] // BLOCK
    slot_ids = jnp.concatenate([kept_ids, cand_ids], axis=1)
    table, position = column_tables(slot_ids % ncols, width)
    vmem = pl.BlockSpec(memory_space=pltpu.VMEM)
    smem = pl.BlockSpec(memory_space=pltpu.SMEM)
    outgoing = pl.pallas_call(
        lambda *refs: pick_kernel(owners, width, *refs),
        out_shape=jax.ShapeDtypeStruct((owners, out_grad.shape[0], width * BLOCK), out_grad.dtype),
        in_specs=[smem, vmem],
        out_specs=vmem,
        name="pick",
    )(table.reshape(-1), out_grad)
    dma = pltpu.SemaphoreType.DMA
    side = math.isqrt(owners // 2)
    my_rows = lax.dynamic_index_in_dim(slot_ids // ncols, owner_index, 0, keepdims=False)
    my_cols = lax.dynamic_index_in_dim(position, owner_index, 0, keepdims=False)
    toks = lax.axis_size("tok")
    kshare, share = KS // toks, cand_ids.shape[1] // toks
    steps = toks // 2
    kept_grad, scores = pl.pallas_call(
        update_kernel,
        out_shape=(
            jax.ShapeDtypeStruct((kshare, BLOCK, BLOCK), jnp.bfloat16),
            jax.ShapeDtypeStruct((1, BLOCK), jnp.float32),
        ),
        in_specs=[smem, smem, vmem, vmem],
        out_specs=(vmem, vmem),
        scratch_shapes=[
            pltpu.VMEM((owners * per, tokens, BLOCK), acts.dtype),
            pltpu.VMEM(outgoing.shape, outgoing.dtype),
            dma((3,)),
            dma((per, side, side)),
            dma((per, side, side)),
            dma((per, side, side)),
            dma((per, side, side)),
            dma((owners,)),
            dma((owners,)),
            pltpu.VMEM((width, tokens, BLOCK), outgoing.dtype),
            pltpu.VMEM((2, steps + 1, kshare, BLOCK, BLOCK), jnp.float32),
            pltpu.VMEM((2, steps + 1, share, BLOCK, BLOCK), jnp.bfloat16),
            dma((2, steps, kshare + share)),
            dma((2, steps, kshare + share)),
            pltpu.VMEM((1, BLOCK), jnp.float32),
            pltpu.VMEM((1, BLOCK), jnp.float32),
            pltpu.VMEM((toks, 1, BLOCK), jnp.float32),
            pltpu.VMEM((owners, toks, 1, BLOCK), jnp.float32),
            dma,
            dma((toks,)),
            dma((toks,)),
            dma((owners,)),
            dma((owners,)),
        ],
        compiler_params=pltpu.CompilerParams(collective_id=0, has_side_effects=True),
        name="update",
    )(my_rows, my_cols, acts, outgoing)
    cand_score = scores[:, :share]
    return (kept_grad[None], cand_score)


def solution(mesh):
    return jax.shard_map(
        local,
        mesh=mesh,
        in_specs=(P("tok", "blk"), P(("tok", "blk"), None), P(), P()),
        out_specs=(P("blk", "tok", None, None), P("blk", "tok")),
        check_vma=False,
    )
```

```python
import math

import jax
import jax.numpy as jnp
from jax import lax
from jax.experimental import pallas as pl
from jax.experimental.pallas import tpu as pltpu
from jax.sharding import PartitionSpec as P

BLOCK = 128
KS = 16


def column_tables(cols, width):
    slots = cols.shape[1]
    same = cols[:, :, None] == cols[:, None, :]
    place = jnp.arange(slots)
    earlier = place[None, :] < place[:, None]
    first = jnp.logical_not(jnp.any(same & earlier[None], axis=2))
    rank = jnp.sum(jnp.where(earlier[None] & first[:, None, :], 1, 0), axis=2)
    position = jnp.sum(jnp.where(same & first[:, None, :], rank[:, None, :], 0), axis=2)
    hit = first[:, None, :] & (rank[:, None, :] == jnp.arange(width)[None, :, None])
    table = jnp.sum(jnp.where(hit, cols[:, None, :], 0), axis=2)
    return table.astype(jnp.int32), position.astype(jnp.int32)


def pick_kernel(owners, width, table_ref, grad_ref, out_ref):
    def one_owner(o, carry):
        for w in range(width):
            col = table_ref[o * width + w]
            out_ref[o, :, w * BLOCK : (w + 1) * BLOCK] = grad_ref[
                :, pl.ds(pl.multiple_of(col * BLOCK, BLOCK), BLOCK)
            ]
        return carry

    lax.fori_loop(0, owners, one_owner, 0)


MESH = pl.DeviceIdType.MESH


def greet(barrier, axis, me, n):
    def one(k, carry):
        pl.semaphore_signal(
            barrier, inc=1, device_id={axis: lax.rem(me + k, n)}, device_id_type=MESH
        )
        return carry

    lax.fori_loop(1, n, one, 0)


def exchange(axis, me, n, src, buf, send, recv, own_sem):
    def copy(k, slot):
        return pltpu.make_async_remote_copy(
            src_ref=src,
            dst_ref=buf.at[slot],
            send_sem=send.at[k],
            recv_sem=recv.at[k],
            device_id={axis: lax.rem(me + k, n)},
            device_id_type=MESH,
        )

    def start_one(k, carry):
        copy(k, me).start()
        return carry

    def finish_one(k, carry):
        arrived = copy(k, lax.rem(me + n - k, n))
        arrived.wait_send()
        arrived.wait_recv()
        return carry

    def start():
        lax.fori_loop(1, n, start_one, 0)
        pltpu.make_async_copy(src, buf.at[me], own_sem).start()

    def finish():
        pltpu.make_async_copy(src, buf.at[me], own_sem).wait()
        lax.fori_loop(1, n, finish_one, 0)

    return start, finish


def gather(
    acts_ref, out_ref, all_ref, in_ref,
    own_sem, acts_send, acts_recv, relay_send, relay_recv, grad_send, grad_recv,
):
    nb = lax.axis_size("blk")
    b = lax.axis_index("blk")
    partner = b + 1 - 2 * lax.rem(b, 2)
    side = acts_send.shape[1]
    per = acts_send.shape[0]

    def remote(src, dst, send, recv, peer):
        return pltpu.make_async_remote_copy(
            src_ref=src,
            dst_ref=dst,
            send_sem=send,
            recv_sem=recv,
            device_id={"blk": peer},
            device_id_type=MESH,
        )

    core = lax.rem(b, 2)
    spot = (lax.rem(b // 2, side), b // (2 * side))
    halves = tuple(
        acts_ref.at[:, pl.ds(h * BLOCK, BLOCK)] for h in range(2)
    )

    def device(h, first, second):
        p = lax.rem(spot[h] + first + side, side)
        q = lax.rem(spot[1 - h] + second + side, side)
        x, y = (p, q) if h == 0 else (q, p)
        return (y * side + x) * 2 + core

    def held(h, i, j):
        return all_ref.at[device(h, -i, -j) * per + h]

    def hop(h, i, j, step):
        i0, j0 = (i - step[0]) % side, (j - step[1]) % side
        here = halves[h] if i0 == 0 and j0 == 0 else held(h, i0, j0)
        return remote(
            here,
            held(h, i0, j0),
            acts_send.at[h, i, j],
            acts_recv.at[h, i, j],
            device(h, step[0], step[1]),
        )

    def landing(h, i, j):
        return remote(held(h, i, j), held(h, i, j), acts_send.at[h, i, j], acts_recv.at[h, i, j], partner)

    def relay_copy(h, i, j):
        here = halves[h] if i == 0 and j == 0 else held(h, i, j)
        return remote(here, held(h, i, j), relay_send.at[h, i, j], relay_recv.at[h, i, j], partner)

    def relay_landing(h, i, j):
        block = all_ref.at[(device(h, -i, -j) + 1 - 2 * core) * per + h]
        return remote(block, block, relay_send.at[h, i, j], relay_recv.at[h, i, j], partner)

    def forward(h, i, j):
        way = 1 if h == 0 else -1
        if j == 0:
            if i == 0:
                hop(h, 1, 0, (1, 0)).start()
                hop(h, side - 1, 0, (-1, 0)).start()
            elif i == way % side:
                hop(h, 2, 0, (way, 0)).start()
            hop(h, i, 1, (0, 1)).start()
            hop(h, i, side - 1, (0, -1)).start()
        elif j == way % side:
            hop(h, i, 2, (0, way)).start()
        relay_copy(h, i, j).start()

    def arrive(h, i, j):
        landing(h, i, j).wait_recv()
        forward(h, i, j)

    def grad_copy(k, slot):
        peer = lax.rem(b + k, nb)
        return remote(out_ref.at[peer], in_ref.at[slot], grad_send.at[k], grad_recv.at[k], peer)

    def start_grad(k, carry):
        grad_copy(k, b).start()
        return carry

    for h in range(2):
        forward(h, 0, 0)
    for i, j in ((1, 0), (3, 0), (0, 1), (0, 3)):
        for h in range(2):
            arrive(h, i, j)
    lax.fori_loop(1, nb, start_grad, 0)
    own_acts = [
        pltpu.make_async_copy(halves[h], all_ref.at[b * per + h], own_sem.at[h]) for h in range(2)
    ]
    own_grad = pltpu.make_async_copy(out_ref.at[b], in_ref.at[b], own_sem.at[2])
    for own in (*own_acts, own_grad):
        own.start()
    later = ((2, 0), (0, 2), (1, 1), (1, 3), (3, 1), (3, 3), (1, 2), (3, 2), (2, 1), (2, 3), (2, 2))
    for i, j in later:
        for h in range(2):
            arrive(h, i, j)

    def finish_grad(k, carry):
        arrived = grad_copy(k, lax.rem(b + nb - k, nb))
        arrived.wait_send()
        arrived.wait_recv()
        return carry

    lax.fori_loop(1, nb, finish_grad, 0)
    for h in range(2):
        for i in range(side):
            for j in range(side):
                if i or j:
                    landing(h, i, j).wait_send()
                relay_landing(h, i, j).wait_send()
                relay_landing(h, i, j).wait_recv()
    for own in (*own_acts, own_grad):
        own.wait()


def update_kernel(
    row_ref, col_ref, acts_ref, out_ref, kept_ref, score_ref,
    all_ref, in_ref, gather_own, acts_send, acts_recv, relay_send, relay_recv, grad_send, grad_recv,
    cols, kept_buf, cand_buf, send_sems, recv_sems,
    norm_buf, mine, line, plane, own_sem, line_send, line_recv, plane_send, plane_recv,
):
    nt, nb = lax.axis_size("tok"), lax.axis_size("blk")
    t, b = lax.axis_index("tok"), lax.axis_index("blk")
    kshare, cshare = kept_buf.shape[2], cand_buf.shape[2]
    blocks = kshare + cshare
    up_hops = nt // 2
    down_hops = nt - 1 - up_hops
    hops = (up_hops, down_hops)
    peers = (lax.rem(t + 1, nt), lax.rem(t + nt - 1, nt))

    barrier = pltpu.get_barrier_semaphore()
    greet(barrier, "tok", t, nt)
    greet(barrier, "blk", b, nb)
    pl.semaphore_wait(barrier, nt + nb - 2)
    gather(
        acts_ref, out_ref, all_ref, in_ref,
        gather_own, acts_send, acts_recv, relay_send, relay_recv, grad_send, grad_recv,
    )
    for w in range(cols.shape[0]):
        rows = in_ref[:, :, w * BLOCK : (w + 1) * BLOCK].astype(jnp.float32)
        cols[w] = rows.reshape(cols.shape[1:]).astype(cols.dtype)

    def product(d, j):
        slot = d * kshare + j if j < kshare else nt * kshare + d * cshare + (j - kshare)
        left = all_ref[row_ref[slot]]
        right = cols[col_ref[slot]]
        return lax.dot_general(
            left, right, (((0,), (0,)), ((), ())), preferred_element_type=jnp.float32
        )

    def home(way, step):
        if way == 0:
            return lax.rem(t + up_hops - step + nt, nt)
        return lax.rem(t + nt - down_hops + step, nt)

    def block(way, step, j):
        if j < kshare:
            return kept_buf.at[way, step, j]
        return cand_buf.at[way, step, j - kshare]

    def copy(way, step, j):
        return pltpu.make_async_remote_copy(
            src_ref=block(way, step, j),
            dst_ref=block(way, step + 1, j),
            send_sem=send_sems.at[way, step, j],
            recv_sem=recv_sems.at[way, step, j],
            device_id={"tok": peers[way]},
            device_id_type=MESH,
        )

    def advance(way, step, j):
        term = product(home(way, step), j)
        copy(way, step - 1, j).wait_recv()
        here = block(way, step, j)
        here[...] = (here[...].astype(jnp.float32) + term).astype(here.dtype)
        copy(way, step, j).start()

    kept, cand = range(kshare), range(kshare, blocks)

    def begin(js):
        for j in js:
            for way in range(2):
                here = block(way, 0, j)
                here[...] = product(home(way, 0), j).astype(here.dtype)
        for j in js:
            for way in range(2):
                copy(way, 0, j).start()

    def both(step, js):
        for j in js:
            for way in range(2):
                advance(way, step, j)

    def total(j):
        value = product(t, j)
        for way in (1, 0):
            copy(way, hops[way] - 1, j).wait_recv()
            value = value + block(way, hops[way], j)[...].astype(jnp.float32)
        return value

    lag = down_hops // 2

    def cand_only(step, carry):
        both(step, cand)
        return carry

    def cand_and_kept(step, carry):
        both(step, cand)
        both(step - lag, kept)
        return carry

    begin(cand)
    lax.fori_loop(1, lag + 1, cand_only, 0)
    begin(kept)
    lax.fori_loop(lag + 1, down_hops, cand_and_kept, 0)
    for step in range(down_hops, up_hops):
        for j in cand:
            advance(0, step, j)
        both(step - lag, kept)

    lane = lax.broadcasted_iota(jnp.int32, norm_buf.shape, 1)
    squares = jnp.zeros(norm_buf.shape, jnp.float32)
    for j in cand:
        value = total(j)
        squares = jnp.where(lane == j - kshare, jnp.sum(value * value), squares)
    norms = jnp.sqrt(squares)
    norm_buf[...] = norms
    own = pltpu.make_async_copy(norm_buf, mine, own_sem)
    own.start()
    own.wait()

    start, finish = exchange("tok", t, nt, mine, line, line_send, line_recv, own_sem)
    start()
    for step in range(up_hops - lag, down_hops):
        both(step, kept)
    finish()
    start, finish = exchange("blk", b, nb, line, plane, plane_send, plane_recv, own_sem)
    start()
    for step in range(down_hops, up_hops):
        for j in kept:
            advance(0, step, j)
    for j in kept:
        kept_ref[j] = total(j).astype(kept_ref.dtype)

    def sent(step, carry):
        for way in range(2):
            for j in range(blocks):
                copy(way, step, j).wait_send()
        return carry

    lax.fori_loop(0, down_hops, sent, 0)
    for step in range(down_hops, up_hops):
        for j in range(blocks):
            copy(0, step, j).wait_send()
    finish()
    score_ref[...] = norms / (jnp.max(plane[...]) + 1e-06)


def local(acts, out_grad, kept_ids, cand_ids):
    owners = lax.axis_size("blk")
    owner_index = lax.axis_index("blk")
    ncols = out_grad.shape[1] // BLOCK
    width = 2 * ((ncols + owners - 1) // owners)
    tokens = acts.shape[0]
    per = acts.shape[1] // BLOCK
    slot_ids = jnp.concatenate([kept_ids, cand_ids], axis=1)
    table, position = column_tables(slot_ids % ncols, width)
    vmem = pl.BlockSpec(memory_space=pltpu.VMEM)
    smem = pl.BlockSpec(memory_space=pltpu.SMEM)
    outgoing = pl.pallas_call(
        lambda *refs: pick_kernel(owners, width, *refs),
        out_shape=jax.ShapeDtypeStruct((owners, out_grad.shape[0], width * BLOCK), out_grad.dtype),
        in_specs=[smem, vmem],
        out_specs=vmem,
        name="pick",
    )(table.reshape(-1), out_grad)
    dma = pltpu.SemaphoreType.DMA
    side = math.isqrt(owners // 2)
    my_rows = lax.dynamic_index_in_dim(slot_ids // ncols, owner_index, 0, keepdims=False)
    my_cols = lax.dynamic_index_in_dim(position, owner_index, 0, keepdims=False)
    toks = lax.axis_size("tok")
    kshare, share = KS // toks, cand_ids.shape[1] // toks
    steps = toks // 2
    kept_grad, scores = pl.pallas_call(
        update_kernel,
        out_shape=(
            jax.ShapeDtypeStruct((kshare, BLOCK, BLOCK), jnp.bfloat16),
            jax.ShapeDtypeStruct((1, BLOCK), jnp.float32),
        ),
        in_specs=[smem, smem, vmem, vmem],
        out_specs=(vmem, vmem),
        scratch_shapes=[
            pltpu.VMEM((owners * per, tokens, BLOCK), acts.dtype),
            pltpu.VMEM(outgoing.shape, outgoing.dtype),
            dma((3,)),
            dma((per, side, side)),
            dma((per, side, side)),
            dma((per, side, side)),
            dma((per, side, side)),
            dma((owners,)),
            dma((owners,)),
            pltpu.VMEM((width, tokens, BLOCK), outgoing.dtype),
            pltpu.VMEM((2, steps + 1, kshare, BLOCK, BLOCK), jnp.float32),
            pltpu.VMEM((2, steps + 1, share, BLOCK, BLOCK), jnp.bfloat16),
            dma((2, steps, kshare + share)),
            dma((2, steps, kshare + share)),
            pltpu.VMEM((1, BLOCK), jnp.float32),
            pltpu.VMEM((1, BLOCK), jnp.float32),
            pltpu.VMEM((toks, 1, BLOCK), jnp.float32),
            pltpu.VMEM((owners, toks, 1, BLOCK), jnp.float32),
            dma,
            dma((toks,)),
            dma((toks,)),
            dma((owners,)),
            dma((owners,)),
        ],
        compiler_params=pltpu.CompilerParams(collective_id=0, has_side_effects=True),
        name="update",
    )(my_rows, my_cols, acts, outgoing)
    cand_score = scores[:, :share]
    return (kept_grad[None], cand_score)


def solution(mesh):
    return jax.shard_map(
        local,
        mesh=mesh,
        in_specs=(P("tok", "blk"), P(("tok", "blk"), None), P(), P()),
        out_specs=(P("blk", "tok", None, None), P("blk", "tok")),
        check_vma=False,
    )
```

```python
import math

import jax
import jax.numpy as jnp
from jax import lax
from jax.experimental import pallas as pl
from jax.experimental.pallas import tpu as pltpu
from jax.sharding import PartitionSpec as P

BLOCK = 128
KS = 16


def column_tables(cols, width):
    slots = cols.shape[1]
    same = cols[:, :, None] == cols[:, None, :]
    place = jnp.arange(slots)
    earlier = place[None, :] < place[:, None]
    first = jnp.logical_not(jnp.any(same & earlier[None], axis=2))
    rank = jnp.sum(jnp.where(earlier[None] & first[:, None, :], 1, 0), axis=2)
    position = jnp.sum(jnp.where(same & first[:, None, :], rank[:, None, :], 0), axis=2)
    hit = first[:, None, :] & (rank[:, None, :] == jnp.arange(width)[None, :, None])
    table = jnp.sum(jnp.where(hit, cols[:, None, :], 0), axis=2)
    return table.astype(jnp.int32), position.astype(jnp.int32)


def pick_kernel(owners, width, table_ref, grad_ref, out_ref):
    def one_owner(o, carry):
        for w in range(width):
            col = table_ref[o * width + w]
            out_ref[o, :, w * BLOCK : (w + 1) * BLOCK] = grad_ref[
                :, pl.ds(pl.multiple_of(col * BLOCK, BLOCK), BLOCK)
            ]
        return carry

    lax.fori_loop(0, owners, one_owner, 0)


MESH = pl.DeviceIdType.MESH


def greet(barrier, axis, me, n):
    def one(k, carry):
        pl.semaphore_signal(
            barrier, inc=1, device_id={axis: lax.rem(me + k, n)}, device_id_type=MESH
        )
        return carry

    lax.fori_loop(1, n, one, 0)


def exchange(axis, me, n, src, buf, send, recv, own_sem):
    def copy(k, slot):
        return pltpu.make_async_remote_copy(
            src_ref=src,
            dst_ref=buf.at[slot],
            send_sem=send.at[k],
            recv_sem=recv.at[k],
            device_id={axis: lax.rem(me + k, n)},
            device_id_type=MESH,
        )

    def start_one(k, carry):
        copy(k, me).start()
        return carry

    def finish_one(k, carry):
        arrived = copy(k, lax.rem(me + n - k, n))
        arrived.wait_send()
        arrived.wait_recv()
        return carry

    def start():
        lax.fori_loop(1, n, start_one, 0)
        pltpu.make_async_copy(src, buf.at[me], own_sem).start()

    def finish():
        pltpu.make_async_copy(src, buf.at[me], own_sem).wait()
        lax.fori_loop(1, n, finish_one, 0)

    return start, finish


def gather(
    acts_ref, out_ref, all_ref, in_ref,
    own_sem, acts_send, acts_recv, relay_send, relay_recv, grad_send, grad_recv,
):
    nb = lax.axis_size("blk")
    b = lax.axis_index("blk")
    partner = b + 1 - 2 * lax.rem(b, 2)
    side = acts_send.shape[1]
    per = acts_send.shape[0]

    def remote(src, dst, send, recv, peer):
        return pltpu.make_async_remote_copy(
            src_ref=src,
            dst_ref=dst,
            send_sem=send,
            recv_sem=recv,
            device_id={"blk": peer},
            device_id_type=MESH,
        )

    core = lax.rem(b, 2)
    spot = (lax.rem(b // 2, side), b // (2 * side))
    halves = tuple(
        acts_ref.at[:, pl.ds(h * BLOCK, BLOCK)] for h in range(2)
    )

    def device(h, first, second):
        p = lax.rem(spot[h] + first + side, side)
        q = lax.rem(spot[1 - h] + second + side, side)
        x, y = (p, q) if h == 0 else (q, p)
        return (y * side + x) * 2 + core

    def held(h, i, j):
        return all_ref.at[device(h, -i, -j) * per + h]

    def hop(h, i, j, step):
        i0, j0 = (i - step[0]) % side, (j - step[1]) % side
        here = halves[h] if i0 == 0 and j0 == 0 else held(h, i0, j0)
        return remote(
            here,
            held(h, i0, j0),
            acts_send.at[h, i, j],
            acts_recv.at[h, i, j],
            device(h, step[0], step[1]),
        )

    def landing(h, i, j):
        return remote(held(h, i, j), held(h, i, j), acts_send.at[h, i, j], acts_recv.at[h, i, j], partner)

    def relay_copy(h, i, j):
        here = halves[h] if i == 0 and j == 0 else held(h, i, j)
        return remote(here, held(h, i, j), relay_send.at[h, i, j], relay_recv.at[h, i, j], partner)

    def relay_landing(h, i, j):
        block = all_ref.at[(device(h, -i, -j) + 1 - 2 * core) * per + h]
        return remote(block, block, relay_send.at[h, i, j], relay_recv.at[h, i, j], partner)

    def forward(h, i, j):
        way = 1 if h == 0 else -1
        if j == 0:
            if i == 0:
                hop(h, 1, 0, (1, 0)).start()
                hop(h, side - 1, 0, (-1, 0)).start()
            elif i == way % side:
                hop(h, 2, 0, (way, 0)).start()
            hop(h, i, 1, (0, 1)).start()
            hop(h, i, side - 1, (0, -1)).start()
        elif j == way % side:
            hop(h, i, 2, (0, way)).start()
        relay_copy(h, i, j).start()

    def arrive(h, i, j):
        landing(h, i, j).wait_recv()
        forward(h, i, j)

    def grad_copy(k, slot):
        peer = lax.rem(b + k, nb)
        return remote(out_ref.at[peer], in_ref.at[slot], grad_send.at[k], grad_recv.at[k], peer)

    def start_grad(k, carry):
        grad_copy(k, b).start()
        return carry

    for h in range(2):
        forward(h, 0, 0)
    for i, j in ((1, 0), (3, 0), (0, 1), (0, 3)):
        for h in range(2):
            arrive(h, i, j)
    lax.fori_loop(1, nb, start_grad, 0)
    own_acts = [
        pltpu.make_async_copy(halves[h], all_ref.at[b * per + h], own_sem.at[h]) for h in range(2)
    ]
    own_grad = pltpu.make_async_copy(out_ref.at[b], in_ref.at[b], own_sem.at[2])
    for own in (*own_acts, own_grad):
        own.start()
    later = ((2, 0), (0, 2), (1, 1), (1, 3), (3, 1), (3, 3), (1, 2), (3, 2), (2, 1), (2, 3), (2, 2))
    for i, j in later:
        for h in range(2):
            arrive(h, i, j)

    def finish_grad(k, carry):
        arrived = grad_copy(k, lax.rem(b + nb - k, nb))
        arrived.wait_send()
        arrived.wait_recv()
        return carry

    lax.fori_loop(1, nb, finish_grad, 0)
    for h in range(2):
        for i in range(side):
            for j in range(side):
                if i or j:
                    landing(h, i, j).wait_send()
                relay_landing(h, i, j).wait_send()
                relay_landing(h, i, j).wait_recv()
    for own in (*own_acts, own_grad):
        own.wait()


def update_kernel(
    row_ref, col_ref, acts_ref, out_ref, kept_ref, score_ref,
    all_ref, in_ref, gather_own, acts_send, acts_recv, relay_send, relay_recv, grad_send, grad_recv,
    cols, kept_buf, cand_buf, send_sems, recv_sems,
    norm_buf, mine, line, plane, own_sem, line_send, line_recv, plane_send, plane_recv,
):
    nt, nb = lax.axis_size("tok"), lax.axis_size("blk")
    t, b = lax.axis_index("tok"), lax.axis_index("blk")
    kshare, cshare = kept_buf.shape[2], cand_buf.shape[2]
    blocks = kshare + cshare
    up_hops = nt // 2
    down_hops = nt - 1 - up_hops
    hops = (up_hops, down_hops)
    peers = (lax.rem(t + 1, nt), lax.rem(t + nt - 1, nt))

    barrier = pltpu.get_barrier_semaphore()
    greet(barrier, "tok", t, nt)
    greet(barrier, "blk", b, nb)
    pl.semaphore_wait(barrier, nt + nb - 2)
    gather(
        acts_ref, out_ref, all_ref, in_ref,
        gather_own, acts_send, acts_recv, relay_send, relay_recv, grad_send, grad_recv,
    )
    for w in range(cols.shape[0]):
        rows = in_ref[:, :, w * BLOCK : (w + 1) * BLOCK].astype(jnp.float32)
        cols[w] = rows.reshape(cols.shape[1:]).astype(cols.dtype)

    def product(d, j):
        slot = d * kshare + j if j < kshare else nt * kshare + d * cshare + (j - kshare)
        left = all_ref[row_ref[slot]]
        right = cols[col_ref[slot]]
        return lax.dot_general(
            left, right, (((0,), (0,)), ((), ())), preferred_element_type=jnp.float32
        )

    def home(way, step):
        if way == 0:
            return lax.rem(t + up_hops - step + nt, nt)
        return lax.rem(t + nt - down_hops + step, nt)

    def block(way, step, j):
        if j < kshare:
            return kept_buf.at[way, step, j]
        return cand_buf.at[way, step, j - kshare]

    def parts(j):
        return range(2 if j < kshare else 1)

    def piece(way, step, j, part):
        if j < kshare:
            return block(way, step, j).at[pl.ds(part * (BLOCK // 2), BLOCK // 2)]
        return block(way, step, j)

    def copy(way, step, j, part):
        return pltpu.make_async_remote_copy(
            src_ref=piece(way, step, j, part),
            dst_ref=piece(way, step + 1, j, part),
            send_sem=send_sems.at[way, step, j + part * blocks],
            recv_sem=recv_sems.at[way, step, j + part * blocks],
            device_id={"tok": peers[way]},
            device_id_type=MESH,
        )

    def advance(way, step, j):
        term = product(home(way, step), j)
        for part in parts(j):
            copy(way, step - 1, j, part).wait_recv()
            here = piece(way, step, j, part)
            rows = here.shape[0]
            mine_here = term[part * rows : (part + 1) * rows]
            here[...] = (here[...].astype(jnp.float32) + mine_here).astype(here.dtype)
            copy(way, step, j, part).start()

    kept, cand = range(kshare), range(kshare, blocks)

    def begin(js):
        for j in js:
            for way in range(2):
                here = block(way, 0, j)
                here[...] = product(home(way, 0), j).astype(here.dtype)
        for j in js:
            for way in range(2):
                for part in parts(j):
                    copy(way, 0, j, part).start()

    def both(step, js):
        for j in js:
            for way in range(2):
                advance(way, step, j)

    def total(j):
        value = product(t, j)
        for way in (1, 0):
            for part in parts(j):
                copy(way, hops[way] - 1, j, part).wait_recv()
            value = value + block(way, hops[way], j)[...].astype(jnp.float32)
        return value

    lag = down_hops // 2

    def cand_only(step, carry):
        both(step, cand)
        return carry

    def cand_and_kept(step, carry):
        both(step, cand)
        both(step - lag, kept)
        return carry

    begin(cand)
    lax.fori_loop(1, lag + 1, cand_only, 0)
    begin(kept)
    lax.fori_loop(lag + 1, down_hops, cand_and_kept, 0)
    for step in range(down_hops, up_hops):
        for j in cand:
            advance(0, step, j)
        both(step - lag, kept)

    lane = lax.broadcasted_iota(jnp.int32, norm_buf.shape, 1)
    squares = jnp.zeros(norm_buf.shape, jnp.float32)
    for j in cand:
        value = total(j)
        squares = jnp.where(lane == j - kshare, jnp.sum(value * value), squares)
    norms = jnp.sqrt(squares)
    norm_buf[...] = norms
    own = pltpu.make_async_copy(norm_buf, mine, own_sem)
    own.start()
    own.wait()

    start, finish = exchange("tok", t, nt, mine, line, line_send, line_recv, own_sem)
    start()
    for step in range(up_hops - lag, down_hops):
        both(step, kept)
    finish()
    start, finish = exchange("blk", b, nb, line, plane, plane_send, plane_recv, own_sem)
    start()
    for step in range(down_hops, up_hops):
        for j in kept:
            advance(0, step, j)
    for j in kept:
        kept_ref[j] = total(j).astype(kept_ref.dtype)

    def sent(step, carry):
        for way in range(2):
            for j in range(blocks):
                for part in parts(j):
                    copy(way, step, j, part).wait_send()
        return carry

    lax.fori_loop(0, down_hops, sent, 0)
    for step in range(down_hops, up_hops):
        for j in range(blocks):
            for part in parts(j):
                copy(0, step, j, part).wait_send()
    finish()
    score_ref[...] = norms / (jnp.max(plane[...]) + 1e-06)


def local(acts, out_grad, kept_ids, cand_ids):
    owners = lax.axis_size("blk")
    owner_index = lax.axis_index("blk")
    ncols = out_grad.shape[1] // BLOCK
    width = 2 * ((ncols + owners - 1) // owners)
    tokens = acts.shape[0]
    per = acts.shape[1] // BLOCK
    slot_ids = jnp.concatenate([kept_ids, cand_ids], axis=1)
    table, position = column_tables(slot_ids % ncols, width)
    vmem = pl.BlockSpec(memory_space=pltpu.VMEM)
    smem = pl.BlockSpec(memory_space=pltpu.SMEM)
    outgoing = pl.pallas_call(
        lambda *refs: pick_kernel(owners, width, *refs),
        out_shape=jax.ShapeDtypeStruct((owners, out_grad.shape[0], width * BLOCK), out_grad.dtype),
        in_specs=[smem, vmem],
        out_specs=vmem,
        name="pick",
    )(table.reshape(-1), out_grad)
    dma = pltpu.SemaphoreType.DMA
    side = math.isqrt(owners // 2)
    my_rows = lax.dynamic_index_in_dim(slot_ids // ncols, owner_index, 0, keepdims=False)
    my_cols = lax.dynamic_index_in_dim(position, owner_index, 0, keepdims=False)
    toks = lax.axis_size("tok")
    kshare, share = KS // toks, cand_ids.shape[1] // toks
    steps = toks // 2
    kept_grad, scores = pl.pallas_call(
        update_kernel,
        out_shape=(
            jax.ShapeDtypeStruct((kshare, BLOCK, BLOCK), jnp.bfloat16),
            jax.ShapeDtypeStruct((1, BLOCK), jnp.float32),
        ),
        in_specs=[smem, smem, vmem, vmem],
        out_specs=(vmem, vmem),
        scratch_shapes=[
            pltpu.VMEM((owners * per, tokens, BLOCK), acts.dtype),
            pltpu.VMEM(outgoing.shape, outgoing.dtype),
            dma((3,)),
            dma((per, side, side)),
            dma((per, side, side)),
            dma((per, side, side)),
            dma((per, side, side)),
            dma((owners,)),
            dma((owners,)),
            pltpu.VMEM((width, tokens, BLOCK), outgoing.dtype),
            pltpu.VMEM((2, steps + 1, kshare, BLOCK, BLOCK), jnp.float32),
            pltpu.VMEM((2, steps + 1, share, BLOCK, BLOCK), jnp.bfloat16),
            dma((2, steps, 2 * kshare + share)),
            dma((2, steps, 2 * kshare + share)),
            pltpu.VMEM((1, BLOCK), jnp.float32),
            pltpu.VMEM((1, BLOCK), jnp.float32),
            pltpu.VMEM((toks, 1, BLOCK), jnp.float32),
            pltpu.VMEM((owners, toks, 1, BLOCK), jnp.float32),
            dma,
            dma((toks,)),
            dma((toks,)),
            dma((owners,)),
            dma((owners,)),
        ],
        compiler_params=pltpu.CompilerParams(collective_id=0, has_side_effects=True),
        name="update",
    )(my_rows, my_cols, acts, outgoing)
    cand_score = scores[:, :share]
    return (kept_grad[None], cand_score)


def solution(mesh):
    return jax.shard_map(
        local,
        mesh=mesh,
        in_specs=(P("tok", "blk"), P(("tok", "blk"), None), P(), P()),
        out_specs=(P("blk", "tok", None, None), P("blk", "tok")),
        check_vma=False,
    )
```

```python
import math

import jax
import jax.numpy as jnp
from jax import lax
from jax.experimental import pallas as pl
from jax.experimental.pallas import tpu as pltpu
from jax.sharding import PartitionSpec as P

BLOCK = 128
KS = 16


def column_tables(cols, width):
    slots = cols.shape[1]
    same = cols[:, :, None] == cols[:, None, :]
    place = jnp.arange(slots)
    earlier = place[None, :] < place[:, None]
    first = jnp.logical_not(jnp.any(same & earlier[None], axis=2))
    rank = jnp.sum(jnp.where(earlier[None] & first[:, None, :], 1, 0), axis=2)
    position = jnp.sum(jnp.where(same & first[:, None, :], rank[:, None, :], 0), axis=2)
    hit = first[:, None, :] & (rank[:, None, :] == jnp.arange(width)[None, :, None])
    table = jnp.sum(jnp.where(hit, cols[:, None, :], 0), axis=2)
    return table.astype(jnp.int32), position.astype(jnp.int32)


def pick_kernel(owners, width, table_ref, grad_ref, out_ref):
    def one_owner(o, carry):
        for w in range(width):
            col = table_ref[o * width + w]
            out_ref[o, :, w * BLOCK : (w + 1) * BLOCK] = grad_ref[
                :, pl.ds(pl.multiple_of(col * BLOCK, BLOCK), BLOCK)
            ]
        return carry

    lax.fori_loop(0, owners, one_owner, 0)


MESH = pl.DeviceIdType.MESH


def greet(barrier, axis, me, n):
    def one(k, carry):
        pl.semaphore_signal(
            barrier, inc=1, device_id={axis: lax.rem(me + k, n)}, device_id_type=MESH
        )
        return carry

    lax.fori_loop(1, n, one, 0)


def exchange(axis, me, n, src, buf, send, recv, own_sem):
    def copy(k, slot):
        return pltpu.make_async_remote_copy(
            src_ref=src,
            dst_ref=buf.at[slot],
            send_sem=send.at[k],
            recv_sem=recv.at[k],
            device_id={axis: lax.rem(me + k, n)},
            device_id_type=MESH,
        )

    def start_one(k, carry):
        copy(k, me).start()
        return carry

    def finish_one(k, carry):
        arrived = copy(k, lax.rem(me + n - k, n))
        arrived.wait_send()
        arrived.wait_recv()
        return carry

    def start():
        lax.fori_loop(1, n, start_one, 0)
        pltpu.make_async_copy(src, buf.at[me], own_sem).start()

    def finish():
        pltpu.make_async_copy(src, buf.at[me], own_sem).wait()
        lax.fori_loop(1, n, finish_one, 0)

    return start, finish


def gather(
    acts_ref, out_ref, all_ref, in_ref,
    own_sem, acts_send, acts_recv, relay_send, relay_recv, grad_send, grad_recv,
):
    nb = lax.axis_size("blk")
    b = lax.axis_index("blk")
    partner = b + 1 - 2 * lax.rem(b, 2)
    side = acts_send.shape[1]
    per = acts_send.shape[0]

    def remote(src, dst, send, recv, peer):
        return pltpu.make_async_remote_copy(
            src_ref=src,
            dst_ref=dst,
            send_sem=send,
            recv_sem=recv,
            device_id={"blk": peer},
            device_id_type=MESH,
        )

    core = lax.rem(b, 2)
    spot = (lax.rem(b // 2, side), b // (2 * side))
    halves = tuple(
        acts_ref.at[:, pl.ds(h * BLOCK, BLOCK)] for h in range(2)
    )

    def device(h, first, second):
        p = lax.rem(spot[h] + first + side, side)
        q = lax.rem(spot[1 - h] + second + side, side)
        x, y = (p, q) if h == 0 else (q, p)
        return (y * side + x) * 2 + core

    def held(h, i, j):
        return all_ref.at[device(h, -i, -j) * per + h]

    def hop(h, i, j, step):
        i0, j0 = (i - step[0]) % side, (j - step[1]) % side
        here = halves[h] if i0 == 0 and j0 == 0 else held(h, i0, j0)
        return remote(
            here,
            held(h, i0, j0),
            acts_send.at[h, i, j],
            acts_recv.at[h, i, j],
            device(h, step[0], step[1]),
        )

    def landing(h, i, j):
        return remote(held(h, i, j), held(h, i, j), acts_send.at[h, i, j], acts_recv.at[h, i, j], partner)

    def relay_copy(h, i, j):
        here = halves[h] if i == 0 and j == 0 else held(h, i, j)
        return remote(here, held(h, i, j), relay_send.at[h, i, j], relay_recv.at[h, i, j], partner)

    def relay_landing(h, i, j):
        block = all_ref.at[(device(h, -i, -j) + 1 - 2 * core) * per + h]
        return remote(block, block, relay_send.at[h, i, j], relay_recv.at[h, i, j], partner)

    def forward(h, i, j):
        way = 1 if h == 0 else -1
        if j == 0:
            if i == 0:
                hop(h, 1, 0, (1, 0)).start()
                hop(h, side - 1, 0, (-1, 0)).start()
            elif i == way % side:
                hop(h, 2, 0, (way, 0)).start()
            hop(h, i, 1, (0, 1)).start()
            hop(h, i, side - 1, (0, -1)).start()
        elif j == way % side:
            hop(h, i, 2, (0, way)).start()
        relay_copy(h, i, j).start()

    def arrive(h, i, j):
        landing(h, i, j).wait_recv()
        forward(h, i, j)

    def grad_copy(k, slot):
        peer = lax.rem(b + k, nb)
        return remote(out_ref.at[peer], in_ref.at[slot], grad_send.at[k], grad_recv.at[k], peer)

    def start_grad(k, carry):
        grad_copy(k, b).start()
        return carry

    for h in range(2):
        forward(h, 0, 0)
    lax.fori_loop(1, nb, start_grad, 0)
    for i, j in ((1, 0), (3, 0), (0, 1), (0, 3)):
        for h in range(2):
            arrive(h, i, j)
    own_acts = [
        pltpu.make_async_copy(halves[h], all_ref.at[b * per + h], own_sem.at[h]) for h in range(2)
    ]
    own_grad = pltpu.make_async_copy(out_ref.at[b], in_ref.at[b], own_sem.at[2])
    for own in (*own_acts, own_grad):
        own.start()
    later = ((2, 0), (0, 2), (1, 1), (1, 3), (3, 1), (3, 3), (1, 2), (3, 2), (2, 1), (2, 3), (2, 2))
    for i, j in later:
        for h in range(2):
            arrive(h, i, j)

    def finish_grad(k, carry):
        arrived = grad_copy(k, lax.rem(b + nb - k, nb))
        arrived.wait_send()
        arrived.wait_recv()
        return carry

    lax.fori_loop(1, nb, finish_grad, 0)
    for h in range(2):
        for i in range(side):
            for j in range(side):
                if i or j:
                    landing(h, i, j).wait_send()
                relay_landing(h, i, j).wait_send()
                relay_landing(h, i, j).wait_recv()
    for own in (*own_acts, own_grad):
        own.wait()


def update_kernel(
    row_ref, col_ref, acts_ref, out_ref, kept_ref, score_ref,
    all_ref, in_ref, gather_own, acts_send, acts_recv, relay_send, relay_recv, grad_send, grad_recv,
    cols, kept_buf, cand_buf, send_sems, recv_sems,
    norm_buf, mine, line, plane, own_sem, line_send, line_recv, plane_send, plane_recv,
):
    nt, nb = lax.axis_size("tok"), lax.axis_size("blk")
    t, b = lax.axis_index("tok"), lax.axis_index("blk")
    kshare, cshare = kept_buf.shape[2], cand_buf.shape[2]
    blocks = kshare + cshare
    up_hops = nt // 2
    down_hops = nt - 1 - up_hops
    hops = (up_hops, down_hops)
    peers = (lax.rem(t + 1, nt), lax.rem(t + nt - 1, nt))

    barrier = pltpu.get_barrier_semaphore()
    greet(barrier, "tok", t, nt)
    greet(barrier, "blk", b, nb)
    pl.semaphore_wait(barrier, nt + nb - 2)
    gather(
        acts_ref, out_ref, all_ref, in_ref,
        gather_own, acts_send, acts_recv, relay_send, relay_recv, grad_send, grad_recv,
    )
    for w in range(cols.shape[0]):
        rows = in_ref[:, :, w * BLOCK : (w + 1) * BLOCK].astype(jnp.float32)
        cols[w] = rows.reshape(cols.shape[1:]).astype(cols.dtype)

    def product(d, j):
        slot = d * kshare + j if j < kshare else nt * kshare + d * cshare + (j - kshare)
        left = all_ref[row_ref[slot]]
        right = cols[col_ref[slot]]
        return lax.dot_general(
            left, right, (((0,), (0,)), ((), ())), preferred_element_type=jnp.float32
        )

    def home(way, step):
        if way == 0:
            return lax.rem(t + up_hops - step + nt, nt)
        return lax.rem(t + nt - down_hops + step, nt)

    def block(way, step, j):
        if j < kshare:
            return kept_buf.at[way, step, j]
        return cand_buf.at[way, step, j - kshare]

    def parts(j):
        return range(2 if j < kshare else 1)

    def piece(way, step, j, part):
        if j < kshare:
            return block(way, step, j).at[pl.ds(part * (BLOCK // 2), BLOCK // 2)]
        return block(way, step, j)

    def copy(way, step, j, part):
        return pltpu.make_async_remote_copy(
            src_ref=piece(way, step, j, part),
            dst_ref=piece(way, step + 1, j, part),
            send_sem=send_sems.at[way, step, j + part * blocks],
            recv_sem=recv_sems.at[way, step, j + part * blocks],
            device_id={"tok": peers[way]},
            device_id_type=MESH,
        )

    def advance(way, step, j):
        term = product(home(way, step), j)
        for part in parts(j):
            copy(way, step - 1, j, part).wait_recv()
            here = piece(way, step, j, part)
            rows = here.shape[0]
            mine_here = term[part * rows : (part + 1) * rows]
            here[...] = (here[...].astype(jnp.float32) + mine_here).astype(here.dtype)
            copy(way, step, j, part).start()

    kept, cand = range(kshare), range(kshare, blocks)

    def begin(js):
        for j in js:
            for way in range(2):
                here = block(way, 0, j)
                here[...] = product(home(way, 0), j).astype(here.dtype)
        for j in js:
            for way in range(2):
                for part in parts(j):
                    copy(way, 0, j, part).start()

    def both(step, js):
        for j in js:
            for way in range(2):
                advance(way, step, j)

    def total(j):
        value = product(t, j)
        for way in (1, 0):
            for part in parts(j):
                copy(way, hops[way] - 1, j, part).wait_recv()
            value = value + block(way, hops[way], j)[...].astype(jnp.float32)
        return value

    lag = down_hops // 2

    def cand_only(step, carry):
        both(step, cand)
        return carry

    def cand_and_kept(step, carry):
        both(step, cand)
        both(step - lag, kept)
        return carry

    begin(cand)
    lax.fori_loop(1, lag + 1, cand_only, 0)
    begin(kept)
    lax.fori_loop(lag + 1, down_hops, cand_and_kept, 0)
    for step in range(down_hops, up_hops):
        for j in cand:
            advance(0, step, j)
        both(step - lag, kept)

    lane = lax.broadcasted_iota(jnp.int32, norm_buf.shape, 1)
    squares = jnp.zeros(norm_buf.shape, jnp.float32)
    for j in cand:
        value = total(j)
        squares = jnp.where(lane == j - kshare, jnp.sum(value * value), squares)
    norms = jnp.sqrt(squares)
    norm_buf[...] = norms
    own = pltpu.make_async_copy(norm_buf, mine, own_sem)
    own.start()
    own.wait()

    start, finish = exchange("tok", t, nt, mine, line, line_send, line_recv, own_sem)
    start()
    for step in range(up_hops - lag, down_hops):
        both(step, kept)
    finish()
    start, finish = exchange("blk", b, nb, line, plane, plane_send, plane_recv, own_sem)
    start()
    for step in range(down_hops, up_hops):
        for j in kept:
            advance(0, step, j)
    for j in kept:
        kept_ref[j] = total(j).astype(kept_ref.dtype)

    def sent(step, carry):
        for way in range(2):
            for j in range(blocks):
                for part in parts(j):
                    copy(way, step, j, part).wait_send()
        return carry

    lax.fori_loop(0, down_hops, sent, 0)
    for step in range(down_hops, up_hops):
        for j in range(blocks):
            for part in parts(j):
                copy(0, step, j, part).wait_send()
    finish()
    score_ref[...] = norms / (jnp.max(plane[...]) + 1e-06)


def local(acts, out_grad, kept_ids, cand_ids):
    owners = lax.axis_size("blk")
    owner_index = lax.axis_index("blk")
    ncols = out_grad.shape[1] // BLOCK
    width = 2 * ((ncols + owners - 1) // owners)
    tokens = acts.shape[0]
    per = acts.shape[1] // BLOCK
    slot_ids = jnp.concatenate([kept_ids, cand_ids], axis=1)
    table, position = column_tables(slot_ids % ncols, width)
    vmem = pl.BlockSpec(memory_space=pltpu.VMEM)
    smem = pl.BlockSpec(memory_space=pltpu.SMEM)
    outgoing = pl.pallas_call(
        lambda *refs: pick_kernel(owners, width, *refs),
        out_shape=jax.ShapeDtypeStruct((owners, out_grad.shape[0], width * BLOCK), out_grad.dtype),
        in_specs=[smem, vmem],
        out_specs=vmem,
        name="pick",
    )(table.reshape(-1), out_grad)
    dma = pltpu.SemaphoreType.DMA
    side = math.isqrt(owners // 2)
    my_rows = lax.dynamic_index_in_dim(slot_ids // ncols, owner_index, 0, keepdims=False)
    my_cols = lax.dynamic_index_in_dim(position, owner_index, 0, keepdims=False)
    toks = lax.axis_size("tok")
    kshare, share = KS // toks, cand_ids.shape[1] // toks
    steps = toks // 2
    kept_grad, scores = pl.pallas_call(
        update_kernel,
        out_shape=(
            jax.ShapeDtypeStruct((kshare, BLOCK, BLOCK), jnp.bfloat16),
            jax.ShapeDtypeStruct((1, BLOCK), jnp.float32),
        ),
        in_specs=[smem, smem, vmem, vmem],
        out_specs=(vmem, vmem),
        scratch_shapes=[
            pltpu.VMEM((owners * per, tokens, BLOCK), acts.dtype),
            pltpu.VMEM(outgoing.shape, outgoing.dtype),
            dma((3,)),
            dma((per, side, side)),
            dma((per, side, side)),
            dma((per, side, side)),
            dma((per, side, side)),
            dma((owners,)),
            dma((owners,)),
            pltpu.VMEM((width, tokens, BLOCK), outgoing.dtype),
            pltpu.VMEM((2, steps + 1, kshare, BLOCK, BLOCK), jnp.float32),
            pltpu.VMEM((2, steps + 1, share, BLOCK, BLOCK), jnp.bfloat16),
            dma((2, steps, 2 * kshare + share)),
            dma((2, steps, 2 * kshare + share)),
            pltpu.VMEM((1, BLOCK), jnp.float32),
            pltpu.VMEM((1, BLOCK), jnp.float32),
            pltpu.VMEM((toks, 1, BLOCK), jnp.float32),
            pltpu.VMEM((owners, toks, 1, BLOCK), jnp.float32),
            dma,
            dma((toks,)),
            dma((toks,)),
            dma((owners,)),
            dma((owners,)),
        ],
        compiler_params=pltpu.CompilerParams(collective_id=0, has_side_effects=True),
        name="update",
    )(my_rows, my_cols, acts, outgoing)
    cand_score = scores[:, :share]
    return (kept_grad[None], cand_score)


def solution(mesh):
    return jax.shard_map(
        local,
        mesh=mesh,
        in_specs=(P("tok", "blk"), P(("tok", "blk"), None), P(), P()),
        out_specs=(P("blk", "tok", None, None), P("blk", "tok")),
        check_vma=False,
    )
```
